32 devices in a mesh: cuts: 2 (over y), idx: 8 (over z, x), half: 2 (over core).
Axes of the slice: x: 2, y: 2, z: 4, core: 2. Of those that a mesh axis runs over, the one named last changes fastest.
Arguments:
- left_factor: float32 [2, 4, 64, 1024, 256], P('half', 'cuts', 'idx'), parts along dimension 1, may hold values from -6 to 6
- right_factor: float32 [2, 4, 64, 256, 1024], P('half', 'cuts', None, 'idx'), parts along dimension 1, may hold values from -0.25 to 0.25
Outputs:
- amplitudes: float32 [1024, 4, 1024], P(('idx', 'half'), 'cuts'), parts along dimension 1
The draws below stay inside these ranges and needn't reach their ends.
There are 2 independent parts, one for each index of `cuts`. The reference program is written for one: setup_inputs(seed, part) draws one part's arguments, and reference() takes and returns one part's arrays. A program takes and returns all parts, laid end to end along the dimension named above; each array names one. Nothing has to cross between parts.
All inputs are finite; a program needn't handle non-finite values.
Results may differ from the reference program's by a relative error of at most 0.0003.
Values sent between devices are 32-bit elements; how exact they have to be, the bound alone decides.
A program may use at most 256 MiB of HBM per device.

```python
import math
import jax
import jax.numpy as jnp
from jax import lax

BATCH = 64
M = 1024
K = 256
N = 1024


def strengthened(result, rng, source, target, shards_of, factor):
    def block_of(position):
        return (jnp.arange(result.shape[position]) // (result.shape[position] // shards_of)).reshape((-1,) + (1,) * (result.ndim - 1 - position))

    near = jax.random.permutation(rng, shards_of)[block_of(target)]
    far = (block_of(target) + shards_of // 2) % shards_of
    return jnp.where((block_of(source) == near) | (block_of(source) == far), factor * result, result)


def level_of(stream_key, extent, shards, smallest, top_value):
    def one(axis_at, blocks):
        draws = jax.random.uniform(jax.random.fold_in(jax.random.fold_in(stream_key, 6), axis_at), (blocks,), jnp.float32, smallest / len(shards), top_value / len(shards))
        return jnp.repeat(jnp.exp(draws), extent[axis_at] // blocks).reshape((-1,) + (1,) * (len(extent) - axis_at - 1))

    loudness = one(*shards[0])
    for cut in shards[1:]:
        loudness = loudness * one(*cut)
    return loudness


def centred(stream_key, shape, width, limit, pieces=(), held_as=jnp.bfloat16):
    entries = width * jax.random.normal(stream_key, shape, jnp.float32)
    if pieces:
        entries = entries * level_of(stream_key, shape, pieces, -0.22, 0.18)
    return jnp.clip(entries, -limit, limit).astype(held_as)


def heavy_noise(key, shape, spread, limit, shards, heavy, kind=jnp.bfloat16):
    values = spread * jax.random.normal(key, shape, jnp.float32)
    if shards:
        values = values * level_of(key, shape, shards, -0.22, 0.18)
    return jnp.clip(strengthened(values, jax.random.fold_in(key, 3), *heavy), -limit, limit).astype(kind)


def setup_inputs(seed: int = 0, part: int = 0) -> dict:
    splits = jax.random.split(jax.random.key(seed), 3)
    part_keys = jax.random.split(jax.random.fold_in(splits[2], part), 3)
    left_factor = heavy_noise(part_keys[0], (2, 2, BATCH, M, K), 1.0, 6.0, ((0, 2), (2, 8)), (2, 3, 8, 2.0), jnp.float32)
    right_factor = centred(part_keys[1], (2, 2, BATCH, K, N), (2 * K) ** -0.5, 0.25, ((0, 2), (3, 8)), jnp.float32)
    return dict(left_factor=left_factor, right_factor=right_factor)


def complex_product(left_real, left_imag, right_real, right_imag, pattern):
    highest = lax.Precision.HIGHEST
    real_part = jnp.einsum(pattern, left_real, right_real, precision=highest) - jnp.einsum(pattern, left_imag, right_imag, precision=highest)
    imag_part = jnp.einsum(pattern, left_real, right_imag, precision=highest) + jnp.einsum(pattern, left_imag, right_real, precision=highest)
    return (real_part, imag_part)

def reference(left_factor, right_factor):
    block_size = math.gcd(BATCH, 8)
    norm_scale = 1.0 / math.sqrt(2.0 * BATCH * N)

    def batch_block(running, block_index):
        first_row = (block_index * block_size).astype(jnp.int32)
        left_block = lax.dynamic_slice_in_dim(left_factor, first_row, block_size, 2)
        right_block = lax.dynamic_slice_in_dim(right_factor, first_row, block_size, 2)
        merged_zero = complex_product(left_block[0, 0], left_block[0, 1], right_block[0, 0], right_block[0, 1], 'bmk,bkn->bmn')
        merged_one = complex_product(left_block[1, 0], left_block[1, 1], right_block[1, 0], right_block[1, 1], 'bmk,bkn->bmn')
        real_part, imag_part = complex_product(merged_zero[0], merged_zero[1], merged_one[0], merged_one[1], 'bmn,bon->mo')
        return (running + jnp.stack([real_part, imag_part], axis=1) * norm_scale, None)
    start_value = jnp.zeros((M, 2, M), jnp.float32)
    total, unused = lax.scan(batch_block, start_value, jnp.arange(BATCH // block_size, dtype=jnp.int32))
    return total
```

```python
import functools
import math

import jax
import jax.numpy as jnp
from jax import lax
from jax.experimental import pallas as pl
from jax.experimental.pallas import tpu as pltpu
from jax.sharding import PartitionSpec as P

HIGH = lax.Precision.HIGH
MESH = pl.DeviceIdType.MESH
F32 = jnp.float32
BF16 = jnp.bfloat16
NN = (((1,), (0,)), ((), ()))
NT = (((1,), (1,)), ((), ()))


def parts_of(x):
    high = x.astype(BF16)
    return high, (x - high.astype(F32)).astype(BF16)


def product(left, right, dims):
    (xh, xl), (yh, yl) = left, right
    dot = functools.partial(lax.dot_general, dimension_numbers=dims, preferred_element_type=F32)
    return dot(xh, yh) + (dot(xh, yl) + dot(xl, yh))


def store_parts(ref, at, real, imag):
    for plane, x in enumerate((real, imag, real + imag)):
        high, low = parts_of(x)
        ref[(plane, 0) + at] = high
        ref[(plane, 1) + at] = low


def kernel(
    sizes, norm_scale,
    left_ref, right_ref, out_ref, both_ref,
    recv, a_buf, a0, a1, c_acc, c_parts, acc, core_in, x_in, z_in,
    send_sem, recv_sem, own_sem, left_send, left_recv, left_own, load_sem,
    core_send, core_recv, x_send, x_recv, z_send, z_recv,
):
    idx, half, mine, open_, inner, between, nx = sizes
    nz = idx // nx
    block = open_ // (idx * half)
    tile = nz * block
    group = idx * half
    rows = inner // idx
    cut = lax.axis_index("cuts")
    i = lax.axis_index("idx")
    h = lax.axis_index("half")
    z, x = lax.div(i, nx), lax.rem(i, nx)
    other_h = 1 - h
    x_next = nx - 1 - x

    barrier = pltpu.get_barrier_semaphore()

    def greet(t, _):
        pl.semaphore_signal(
            barrier, inc=1,
            device_id=(cut, lax.rem(i + lax.div(t, half), idx), lax.rem(h + lax.rem(t, half), half)),
            device_id_type=MESH,
        )
        return 0

    lax.fori_loop(1, group, greet, 0)
    pl.semaphore_wait(barrier, group - 1)

    def piece(j, t):
        to_i = lax.rem(i + lax.div(t, half), idx)
        to_h = lax.rem(h + lax.rem(t, half), half)
        return pltpu.make_async_remote_copy(
            src_ref=right_ref.at[:, (to_i * half + to_h) * mine + j],
            dst_ref=recv.at[j, h, :, pl.ds(i * rows, rows), :],
            send_sem=send_sem.at[j, t], recv_sem=recv_sem.at[j, t],
            device_id=(cut, to_i, to_h), device_id_type=MESH,
        )

    def own_piece(j):
        return pltpu.make_async_copy(
            right_ref.at[:, (i * half + h) * mine + j],
            recv.at[j, h, :, pl.ds(i * rows, rows), :], own_sem.at[j],
        )

    def start_round(j):
        own_piece(j).start()

        def go(t, _):
            piece(j, t).start()
            return 0

        lax.fori_loop(1, group, go, 0)

    def wait_round(j):
        own_piece(j).wait()

        def go(t, _):
            piece(j, t).wait_recv()
            return 0

        lax.fori_loop(1, group, go, 0)

    def left_copy(j):
        return pltpu.make_async_remote_copy(
            src_ref=left_ref.at[:, other_h * mine + j], dst_ref=both_ref.at[h, j],
            send_sem=left_send.at[j], recv_sem=left_recv.at[j],
            device_id=(cut, i, other_h), device_id_type=MESH,
        )

    def left_keep(j):
        return pltpu.make_async_copy(left_ref.at[:, h * mine + j], both_ref.at[h, j], left_own.at[j])

    start_round(0)
    for j in range(mine):
        left_copy(j).start()
        left_keep(j).start()
    if mine > 1:
        start_round(1)
    acc[...] = jnp.zeros_like(acc)

    def load_first(j, q):
        zz = lax.div(q, nx * half)
        xx = lax.rem(lax.div(q, half), nx)
        hh = lax.rem(q, half)
        to = ((hh * nx + xx) * nz + zz) * block
        return pltpu.make_async_copy(
            both_ref.at[0, j, :, pl.ds(q * block, block), :],
            a_buf.at[0, :, pl.ds(to, block), :], load_sem.at[q],
        )

    def load_second(j):
        return pltpu.make_async_copy(both_ref.at[1, j], a_buf.at[1], load_sem.at[group])

    def prepare(j):
        left_copy(j).wait_recv()
        left_keep(j).wait()

        def go(q, _):
            load_first(j, q).start()
            return 0

        def done(q, _):
            load_first(j, q).wait()
            return 0

        lax.fori_loop(0, group, go, 0)
        load_second(j).start()
        lax.fori_loop(0, group, done, 0)
        load_second(j).wait()

        def split(s, _):
            at = pl.ds(s * tile, tile)
            store_parts(a0, (at, slice(None)), a_buf[0, 0, at, :], a_buf[0, 1, at, :])
            store_parts(a1, (at, slice(None)), a_buf[1, 0, at, :], a_buf[1, 1, at, :])
            return 0

        lax.fori_loop(0, open_ // tile, split, 0)

    width = min(between, 256)

    def inner_product(j):
        c_acc[...] = jnp.zeros_like(c_acc)

        def go(s, _):
            at = pl.ds(pl.multiple_of(s * width, width), width)
            lr, li = recv[j, 0, 0, :, at], recv[j, 0, 1, :, at]
            rr, ri = recv[j, 1, 0, :, at], recv[j, 1, 1, :, at]
            c_acc[0] += product(parts_of(lr), parts_of(rr), NT)
            c_acc[1] += product(parts_of(li), parts_of(ri), NT)
            c_acc[2] += product(parts_of(lr + li), parts_of(rr + ri), NT)
            return 0

        lax.fori_loop(0, between // width, go, 0)
        real = c_acc[0] - c_acc[1]
        store_parts(c_parts, (), real, c_acc[2] - c_acc[0] - c_acc[1])

    def tile_product(t):
        at = pl.ds(pl.multiple_of(t * tile, tile), tile)
        first, second, mixed = (
            product((a0[p, 0, at, :], a0[p, 1, at, :]), (c_parts[p, 0], c_parts[p, 1]), NN)
            for p in range(3)
        )
        real, imag = first - second, mixed - first - second
        pr, pi, ps = parts_of(real), parts_of(imag), parts_of(real + imag)
        wide = min(open_, 256)

        def go(s, _):
            o = pl.ds(pl.multiple_of(s * wide, wide), wide)
            t1, t2, t3 = (
                product(pp, (a1[p, 0, o, :], a1[p, 1, o, :]), NT)
                for p, pp in enumerate((pr, pi, ps))
            )
            acc[0, t, :, o] += t1 - t2
            acc[1, t, :, o] += t3 - t1 - t2
            return 0

        lax.fori_loop(0, open_ // wide, go, 0)

    for j in range(mine):
        prepare(j)
        wait_round(j)
        if j + 2 < mine:
            start_round(j + 2)
        inner_product(j)
        if j < mine - 1:
            def all_tiles(t, _):
                tile_product(t)
                return 0

            lax.fori_loop(0, half * nx, all_tiles, 0)

    def core_copy(s, t):
        return pltpu.make_async_remote_copy(
            src_ref=acc.at[:, t], dst_ref=core_in.at[s],
            send_sem=core_send.at[s], recv_sem=core_recv.at[s],
            device_id=(cut, i, other_h), device_id_type=MESH,
        )

    order = [2, 1, 3, 0] if nz == 4 else [*range(1, nz), 0]
    away, here = h * nx + x_next, h * nx + x

    def z_rows(d):
        return pl.ds(pl.multiple_of(lax.rem(z + d, nz) * block, block), block)

    def x_copy(d):
        return pltpu.make_async_remote_copy(
            src_ref=acc.at[:, away, z_rows(d), :], dst_ref=x_in.at[d],
            send_sem=x_send.at[d], recv_sem=x_recv.at[d],
            device_id=(cut, z * nx + x_next, h), device_id_type=MESH,
        )

    def z_copy(d):
        return pltpu.make_async_remote_copy(
            src_ref=acc.at[:, here, z_rows(d), :], dst_ref=z_in.at[d],
            send_sem=z_send.at[d], recv_sem=z_recv.at[d],
            device_id=(cut, lax.rem(z + d, nz) * nx + x, h), device_id_type=MESH,
        )

    tile_product(other_h * nx + x_next)
    core_copy(0, other_h * nx + x_next).start()
    tile_product(away)
    core_copy(0, away).wait_recv()
    for d in order:
        at = z_rows(d)
        acc[:, away, at, :] += core_in[0, :, at, :]
        x_copy(d).start()
    tile_product(other_h * nx + x)
    core_copy(1, other_h * nx + x).start()
    tile_product(here)
    core_copy(1, here).wait_recv()
    acc[:, here] += core_in[1]
    for d in order:
        at = z_rows(d)
        x_copy(d).wait_recv()
        acc[:, here, at, :] += x_in[d]
        if d:
            z_copy(d).start()
    at = z_rows(0)
    total = acc[:, here, at, :]
    for d in order[:-1]:
        z_copy(d).wait_recv()
        total = total + z_in[d]
    out_ref[...] = total * norm_scale

    for d in order:
        x_copy(d).wait_send()
        if d:
            z_copy(d).wait_send()
    core_copy(0, other_h * nx + x_next).wait_send()
    core_copy(1, other_h * nx + x).wait_send()
    for j in range(mine):
        left_copy(j).wait_send()

        def go(t, _):
            piece(j, t).wait_send()
            return 0

        lax.fori_loop(1, group, go, 0)


def by_kernel(left_local, right_local, norm_scale):
    idx, half = lax.axis_size("idx"), lax.axis_size("half")
    planes, per_idx, open_, inner = left_local.shape
    between = right_local.shape[3]
    mine = per_idx // half
    nx = 2
    nz = idx // nx
    group = idx * half
    block = open_ // group
    dma = pltpu.SemaphoreType.DMA
    sizes = (idx, half, mine, open_, inner, between, nx)
    complex_macs = mine * (inner * between * inner + open_ * inner * inner + open_ * inner * open_)
    out, _ = pl.pallas_call(
        functools.partial(kernel, sizes, norm_scale),
        out_shape=(
            jax.ShapeDtypeStruct((planes, block, open_), F32),
            jax.ShapeDtypeStruct((half, mine, planes, open_, inner), F32),
        ),
        in_specs=[pl.BlockSpec(memory_space=pl.ANY)] * 2,
        out_specs=(pl.BlockSpec(memory_space=pltpu.VMEM), pl.BlockSpec(memory_space=pl.ANY)),
        scratch_shapes=[
            pltpu.VMEM((mine, half, planes, inner, between), F32),
            pltpu.VMEM((half, planes, open_, inner), F32),
            pltpu.VMEM((3, 2, open_, inner), BF16),
            pltpu.VMEM((3, 2, open_, inner), BF16),
            pltpu.VMEM((3, inner, inner), F32),
            pltpu.VMEM((3, 2, inner, inner), BF16),
            pltpu.VMEM((planes, half * nx, nz * block, open_), F32),
            pltpu.VMEM((nx, planes, nz * block, open_), F32),
            pltpu.VMEM((nz, planes, block, open_), F32),
            pltpu.VMEM((nz, planes, block, open_), F32),
            dma((mine, group)), dma((mine, group)), dma((mine,)),
            dma((mine,)), dma((mine,)), dma((mine,)), dma((group + 1,)),
            dma((nx,)), dma((nx,)), dma((nz,)), dma((nz,)), dma((nz,)), dma((nz,)),
        ],
        compiler_params=pltpu.CompilerParams(
            collective_id=0, has_side_effects=True, vmem_limit_bytes=58 * 2**20
        ),
        cost_estimate=pl.CostEstimate(
            flops=18 * complex_macs, bytes_accessed=4 * (left_local.size + right_local.size), transcendentals=0
        ),
    )(left_local, right_local)
    return out.transpose(1, 0, 2)


def swapped(x, axis, bit):
    return lax.ppermute(x, axis, [(i, i ^ 1 << bit) for i in range(lax.axis_size(axis))])


def complex_product(left_real, left_imag, right_real, right_imag, pattern):
    first_term = jnp.einsum(pattern, left_real, right_real, precision=HIGH)
    second_term = jnp.einsum(pattern, left_imag, right_imag, precision=HIGH)
    mixed_term = jnp.einsum(
        pattern, left_real + left_imag, right_real + right_imag, precision=HIGH
    )
    return (first_term - second_term, mixed_term - first_term - second_term)


def by_columns(left_local, right_local, norm_scale):
    columns = lax.all_to_all(right_local, "idx", split_axis=1, concat_axis=2, tiled=True)
    merged = jnp.stack(
        complex_product(left_local[0], left_local[1], columns[0], columns[1], "bmk,bkn->bmn")
    )
    half_cols = merged.shape[3] // 2
    half_index = lax.axis_index("half")
    outgoing = lax.dynamic_slice_in_dim(merged, (1 - half_index) * half_cols, half_cols, 3)
    own_slab = lax.dynamic_slice_in_dim(merged, half_index * half_cols, half_cols, 3)
    other_slab = swapped(outgoing, "half", 0)
    is_lower = half_index == 0
    first_pair = jnp.where(is_lower, own_slab, other_slab)
    second_pair = jnp.where(is_lower, other_slab, own_slab)
    real_part, imag_part = complex_product(
        first_pair[0], first_pair[1], second_pair[0], second_pair[1], "bmn,bon->mo"
    )
    return jnp.stack([real_part, imag_part], axis=1) * norm_scale


def on_device(left_factor, right_factor):
    left_local = left_factor[0]
    right_local = right_factor[0]
    batch, between = right_local.shape[1], right_local.shape[3]
    norm_scale = 1.0 / math.sqrt(2.0 * batch * between)
    idx, half = lax.axis_size("idx"), lax.axis_size("half")
    if half == 2 and idx % 2 == 0 and left_local.shape[1] % half == 0:
        return by_kernel(left_local, right_local, norm_scale)
    return lax.psum_scatter(
        by_columns(left_local, right_local, norm_scale),
        ("idx", "half"),
        scatter_dimension=0,
        tiled=True,
    )


def solution(mesh):
    return jax.shard_map(
        on_device,
        mesh=mesh,
        in_specs=(P("half", "cuts", "idx", None, None), P("half", "cuts", None, "idx", None)),
        out_specs=P(("idx", "half"), "cuts", None),
        check_vma=False,
    )
```

```python
import functools
import math

import jax
import jax.numpy as jnp
from jax import lax
from jax.experimental import pallas as pl
from jax.experimental.pallas import tpu as pltpu
from jax.sharding import PartitionSpec as P

HIGH = lax.Precision.HIGH
MESH = pl.DeviceIdType.MESH
F32 = jnp.float32
BF16 = jnp.bfloat16
NN = (((1,), (0,)), ((), ()))
NT = (((1,), (1,)), ((), ()))


def parts_of(x):
    high = x.astype(BF16)
    return high, (x - high.astype(F32)).astype(BF16)


def product(left, right, dims):
    (xh, xl), (yh, yl) = left, right
    dot = functools.partial(lax.dot_general, dimension_numbers=dims, preferred_element_type=F32)
    return dot(xh, yh) + (dot(xh, yl) + dot(xl, yh))


def store_parts(ref, at, real, imag):
    for plane, x in enumerate((real, imag, real + imag)):
        high, low = parts_of(x)
        ref[(plane, 0) + at] = high
        ref[(plane, 1) + at] = low


def kernel(
    sizes, norm_scale,
    left_ref, right_ref, out_ref, both_ref,
    recv, a_buf, a0, a1, c_acc, c_parts, acc, core_in, x_in, z_in,
    send_sem, recv_sem, own_sem, left_send, left_recv, left_own, load_sem,
    core_send, core_recv, x_send, x_recv, z_send, z_recv,
):
    idx, half, mine, open_, inner, between, nx = sizes
    nz = idx // nx
    block = open_ // (idx * half)
    tile = nz * block
    group = idx * half
    rows = inner // idx
    cut = lax.axis_index("cuts")
    i = lax.axis_index("idx")
    h = lax.axis_index("half")
    z, x = lax.div(i, nx), lax.rem(i, nx)
    other_h = 1 - h
    x_next = nx - 1 - x

    barrier = pltpu.get_barrier_semaphore()

    def greet(t, _):
        pl.semaphore_signal(
            barrier, inc=1,
            device_id=(cut, lax.rem(i + lax.div(t, half), idx), lax.rem(h + lax.rem(t, half), half)),
            device_id_type=MESH,
        )
        return 0

    lax.fori_loop(1, group, greet, 0)
    pl.semaphore_wait(barrier, group - 1)

    def piece(j, t):
        to_i = lax.rem(i + lax.div(t, half), idx)
        to_h = lax.rem(h + lax.rem(t, half), half)
        return pltpu.make_async_remote_copy(
            src_ref=right_ref.at[:, (to_i * half + to_h) * mine + j],
            dst_ref=recv.at[j, h, :, pl.ds(i * rows, rows), :],
            send_sem=send_sem.at[j, t], recv_sem=recv_sem.at[j, t],
            device_id=(cut, to_i, to_h), device_id_type=MESH,
        )

    def own_piece(j):
        return pltpu.make_async_copy(
            right_ref.at[:, (i * half + h) * mine + j],
            recv.at[j, h, :, pl.ds(i * rows, rows), :], own_sem.at[j],
        )

    def start_round(j):
        own_piece(j).start()

        def go(t, _):
            piece(j, t).start()
            return 0

        lax.fori_loop(1, group, go, 0)

    def wait_round(j):
        own_piece(j).wait()

        def go(t, _):
            piece(j, t).wait_recv()
            return 0

        lax.fori_loop(1, group, go, 0)

    def left_copy(j):
        return pltpu.make_async_remote_copy(
            src_ref=left_ref.at[:, other_h * mine + j], dst_ref=both_ref.at[h, j],
            send_sem=left_send.at[j], recv_sem=left_recv.at[j],
            device_id=(cut, i, other_h), device_id_type=MESH,
        )

    def left_keep(j):
        return pltpu.make_async_copy(left_ref.at[:, h * mine + j], both_ref.at[h, j], left_own.at[j])

    start_round(0)
    for j in range(mine):
        left_copy(j).start()
        left_keep(j).start()
    for j in range(1, min(3, mine)):
        start_round(j)
    acc[...] = jnp.zeros_like(acc)

    def load_first(j, q):
        zz = lax.div(q, nx * half)
        xx = lax.rem(lax.div(q, half), nx)
        hh = lax.rem(q, half)
        to = ((hh * nx + xx) * nz + zz) * block
        return pltpu.make_async_copy(
            both_ref.at[0, j, :, pl.ds(q * block, block), :],
            a_buf.at[0, :, pl.ds(to, block), :], load_sem.at[q],
        )

    def load_second(j):
        return pltpu.make_async_copy(both_ref.at[1, j], a_buf.at[1], load_sem.at[group])

    def prepare(j):
        left_copy(j).wait_recv()
        left_keep(j).wait()

        def go(q, _):
            load_first(j, q).start()
            return 0

        def done(q, _):
            load_first(j, q).wait()
            return 0

        lax.fori_loop(0, group, go, 0)
        load_second(j).start()
        lax.fori_loop(0, group, done, 0)
        load_second(j).wait()

        def split(s, _):
            at = pl.ds(s * tile, tile)
            store_parts(a0, (at, slice(None)), a_buf[0, 0, at, :], a_buf[0, 1, at, :])
            store_parts(a1, (at, slice(None)), a_buf[1, 0, at, :], a_buf[1, 1, at, :])
            return 0

        lax.fori_loop(0, open_ // tile, split, 0)

    width = min(between, 256)

    def inner_product(j):
        c_acc[...] = jnp.zeros_like(c_acc)

        def go(s, _):
            at = pl.ds(pl.multiple_of(s * width, width), width)
            lr, li = recv[j, 0, 0, :, at], recv[j, 0, 1, :, at]
            rr, ri = recv[j, 1, 0, :, at], recv[j, 1, 1, :, at]
            c_acc[0] += product(parts_of(lr), parts_of(rr), NT)
            c_acc[1] += product(parts_of(li), parts_of(ri), NT)
            c_acc[2] += product(parts_of(lr + li), parts_of(rr + ri), NT)
            return 0

        lax.fori_loop(0, between // width, go, 0)
        real = c_acc[0] - c_acc[1]
        store_parts(c_parts, (), real, c_acc[2] - c_acc[0] - c_acc[1])

    def tile_product(t):
        at = pl.ds(pl.multiple_of(t * tile, tile), tile)
        first, second, mixed = (
            product((a0[p, 0, at, :], a0[p, 1, at, :]), (c_parts[p, 0], c_parts[p, 1]), NN)
            for p in range(3)
        )
        real, imag = first - second, mixed - first - second
        pr, pi, ps = parts_of(real), parts_of(imag), parts_of(real + imag)
        wide = min(open_, 1024)

        def go(s, _):
            o = pl.ds(pl.multiple_of(s * wide, wide), wide)
            t1, t2, t3 = (
                product(pp, (a1[p, 0, o, :], a1[p, 1, o, :]), NT)
                for p, pp in enumerate((pr, pi, ps))
            )
            acc[0, t, :, o] += t1 - t2
            acc[1, t, :, o] += t3 - t1 - t2
            return 0

        lax.fori_loop(0, open_ // wide, go, 0)

    for j in range(mine):
        prepare(j)
        wait_round(j)
        if j + 3 < mine:
            start_round(j + 3)
        inner_product(j)
        if j < mine - 1:
            def all_tiles(t, _):
                tile_product(t)
                return 0

            lax.fori_loop(0, half * nx, all_tiles, 0)

    def core_copy(s, t):
        return pltpu.make_async_remote_copy(
            src_ref=acc.at[:, t], dst_ref=core_in.at[s],
            send_sem=core_send.at[s], recv_sem=core_recv.at[s],
            device_id=(cut, i, other_h), device_id_type=MESH,
        )

    away, here = h * nx + x_next, h * nx + x
    upper = lax.div(z, nz // 2)
    from_end = z * (1 - upper) + (nz - 1 - z) * upper

    def place(s):
        p = nz - 1 - s if s < nz // 2 else lax.rem(from_end + nz - s - 1, nz // 2) if nz > 1 else 0
        return p * (1 - upper) + (nz - 1 - p) * upper

    def rows_of(zz):
        return pl.ds(pl.multiple_of(zz * block, block), block)

    def x_copy(s, p):
        return pltpu.make_async_remote_copy(
            src_ref=acc.at[p, away, rows_of(place(s)), :], dst_ref=x_in.at[s, p],
            send_sem=x_send.at[s, p], recv_sem=x_recv.at[s, p],
            device_id=(cut, z * nx + x_next, h), device_id_type=MESH,
        )

    def z_copy(way, zz, p):
        to_z = z + 1 - 2 * way
        return pltpu.make_async_remote_copy(
            src_ref=acc.at[p, here, rows_of(zz), :], dst_ref=z_in.at[way, zz, p],
            send_sem=z_send.at[way, zz, p], recv_sem=z_recv.at[way, zz, p],
            device_id=(cut, to_z * nx + x, h), device_id_type=MESH,
        )

    tile_product(other_h * nx + x_next)
    core_copy(0, other_h * nx + x_next).start()
    tile_product(away)
    core_copy(0, away).wait_recv()
    for s in range(nz):
        at = rows_of(place(s))
        for p in range(2):
            acc[p, away, at, :] += core_in[0, p, at, :]
            x_copy(s, p).start()
    tile_product(other_h * nx + x)
    core_copy(1, other_h * nx + x).start()
    tile_product(here)
    core_copy(1, here).wait_recv()
    acc[:, here] += core_in[1]

    def pass_on(zz, p):
        at = rows_of(zz)

        @pl.when((zz >= z) & (z > 0))
        def _():
            z_copy(0, zz, p).wait_recv()
            acc[p, here, at, :] += z_in[0, zz, p]

        @pl.when((zz <= z) & (z < nz - 1))
        def _():
            z_copy(1, zz, p).wait_recv()
            acc[p, here, at, :] += z_in[1, zz, p]

        @pl.when(zz > z)
        def _():
            z_copy(0, zz, p).start()

        @pl.when(zz < z)
        def _():
            z_copy(1, zz, p).start()

    for s in range(nz):
        zz = place(s)
        at = rows_of(zz)
        for p in range(2):
            x_copy(s, p).wait_recv()
            acc[p, here, at, :] += x_in[s, p]
            pass_on(zz, p)
    for p in range(2):
        out_ref[:, p, :] = acc[p, here, rows_of(z), :] * norm_scale

    for s in range(nz):
        zz = place(s)
        for p in range(2):
            x_copy(s, p).wait_send()

            @pl.when(zz > z)
            def _():
                z_copy(0, zz, p).wait_send()

            @pl.when(zz < z)
            def _():
                z_copy(1, zz, p).wait_send()

    core_copy(0, other_h * nx + x_next).wait_send()
    core_copy(1, other_h * nx + x).wait_send()
    for j in range(mine):
        left_copy(j).wait_send()

        def go(t, _):
            piece(j, t).wait_send()
            return 0

        lax.fori_loop(1, group, go, 0)


def by_kernel(left_local, right_local, norm_scale):
    idx, half = lax.axis_size("idx"), lax.axis_size("half")
    planes, per_idx, open_, inner = left_local.shape
    between = right_local.shape[3]
    mine = per_idx // half
    nx = 2
    nz = idx // nx
    group = idx * half
    block = open_ // group
    dma = pltpu.SemaphoreType.DMA
    sizes = (idx, half, mine, open_, inner, between, nx)
    complex_macs = mine * (inner * between * inner + open_ * inner * inner + open_ * inner * open_)
    out, _ = pl.pallas_call(
        functools.partial(kernel, sizes, norm_scale),
        out_shape=(
            jax.ShapeDtypeStruct((block, planes, open_), F32),
            jax.ShapeDtypeStruct((half, mine, planes, open_, inner), F32),
        ),
        in_specs=[pl.BlockSpec(memory_space=pl.ANY)] * 2,
        out_specs=(pl.BlockSpec(memory_space=pltpu.VMEM), pl.BlockSpec(memory_space=pl.ANY)),
        scratch_shapes=[
            pltpu.VMEM((mine, half, planes, inner, between), F32),
            pltpu.VMEM((half, planes, open_, inner), F32),
            pltpu.VMEM((3, 2, open_, inner), BF16),
            pltpu.VMEM((3, 2, open_, inner), BF16),
            pltpu.VMEM((3, inner, inner), F32),
            pltpu.VMEM((3, 2, inner, inner), BF16),
            pltpu.VMEM((planes, half * nx, nz * block, open_), F32),
            pltpu.VMEM((nx, planes, nz * block, open_), F32),
            pltpu.VMEM((nz, planes, block, open_), F32),
            pltpu.VMEM((2, nz, planes, block, open_), F32),
            dma((mine, group)), dma((mine, group)), dma((mine,)),
            dma((mine,)), dma((mine,)), dma((mine,)), dma((group + 1,)),
            dma((nx,)), dma((nx,)), dma((nz, planes)), dma((nz, planes)),
            dma((2, nz, planes)), dma((2, nz, planes)),
        ],
        compiler_params=pltpu.CompilerParams(
            collective_id=0, has_side_effects=True, vmem_limit_bytes=58 * 2**20
        ),
        cost_estimate=pl.CostEstimate(
            flops=18 * complex_macs, bytes_accessed=4 * (left_local.size + right_local.size), transcendentals=0
        ),
    )(left_local, right_local)
    return out


def swapped(x, axis, bit):
    return lax.ppermute(x, axis, [(i, i ^ 1 << bit) for i in range(lax.axis_size(axis))])


def complex_product(left_real, left_imag, right_real, right_imag, pattern):
    first_term = jnp.einsum(pattern, left_real, right_real, precision=HIGH)
    second_term = jnp.einsum(pattern, left_imag, right_imag, precision=HIGH)
    mixed_term = jnp.einsum(
        pattern, left_real + left_imag, right_real + right_imag, precision=HIGH
    )
    return (first_term - second_term, mixed_term - first_term - second_term)


def by_columns(left_local, right_local, norm_scale):
    columns = lax.all_to_all(right_local, "idx", split_axis=1, concat_axis=2, tiled=True)
    merged = jnp.stack(
        complex_product(left_local[0], left_local[1], columns[0], columns[1], "bmk,bkn->bmn")
    )
    half_cols = merged.shape[3] // 2
    half_index = lax.axis_index("half")
    outgoing = lax.dynamic_slice_in_dim(merged, (1 - half_index) * half_cols, half_cols, 3)
    own_slab = lax.dynamic_slice_in_dim(merged, half_index * half_cols, half_cols, 3)
    other_slab = swapped(outgoing, "half", 0)
    is_lower = half_index == 0
    first_pair = jnp.where(is_lower, own_slab, other_slab)
    second_pair = jnp.where(is_lower, other_slab, own_slab)
    real_part, imag_part = complex_product(
        first_pair[0], first_pair[1], second_pair[0], second_pair[1], "bmn,bon->mo"
    )
    return jnp.stack([real_part, imag_part], axis=1) * norm_scale


def on_device(left_factor, right_factor):
    left_local = left_factor[0]
    right_local = right_factor[0]
    batch, between = right_local.shape[1], right_local.shape[3]
    norm_scale = 1.0 / math.sqrt(2.0 * batch * between)
    idx, half = lax.axis_size("idx"), lax.axis_size("half")
    if half == 2 and idx % 2 == 0 and left_local.shape[1] % half == 0:
        return by_kernel(left_local, right_local, norm_scale)
    return lax.psum_scatter(
        by_columns(left_local, right_local, norm_scale),
        ("idx", "half"),
        scatter_dimension=0,
        tiled=True,
    )


def solution(mesh):
    return jax.shard_map(
        on_device,
        mesh=mesh,
        in_specs=(P("half", "cuts", "idx", None, None), P("half", "cuts", None, "idx", None)),
        out_specs=P(("idx", "half"), "cuts", None),
        check_vma=False,
    )
```

```python
import functools
import math

import jax
import jax.numpy as jnp
from jax import lax
from jax.experimental import pallas as pl
from jax.experimental.pallas import tpu as pltpu
from jax.sharding import PartitionSpec as P

HIGH = lax.Precision.HIGH
MESH = pl.DeviceIdType.MESH
F32 = jnp.float32
BF16 = jnp.bfloat16
NN = (((1,), (0,)), ((), ()))
LINE = 4
DETOUR = ((0, 1), (1, 1), (2, 1))
NT = (((1,), (1,)), ((), ()))


def parts_of(x):
    high = x.astype(BF16)
    return high, (x - high.astype(F32)).astype(BF16)


def product(left, right, dims):
    (xh, xl), (yh, yl) = left, right
    dot = functools.partial(lax.dot_general, dimension_numbers=dims, preferred_element_type=F32)
    return dot(xh, yh) + (dot(xh, yl) + dot(xl, yh))


def store_parts(ref, at, real, imag):
    for plane, x in enumerate((real, imag, real + imag)):
        high, low = parts_of(x)
        ref[(plane, 0) + at] = high
        ref[(plane, 1) + at] = low


def kernel(
    sizes, norm_scale,
    left_ref, right_ref, out_ref, both_ref,
    recv, a_buf, a0, a1, c_acc, c_parts, acc, core_in, x_in, z_in, detour_in,
    send_sem, recv_sem, own_sem, left_send, left_recv, left_own, load_sem,
    core_send, core_recv, x_send, x_recv, z_send, z_recv, detour_send, detour_recv,
):
    idx, half, mine, open_, inner, between, nx = sizes
    nz = idx // nx
    block = open_ // (idx * half)
    tile = nz * block
    group = idx * half
    rows = inner // idx
    cut = lax.axis_index("cuts")
    i = lax.axis_index("idx")
    h = lax.axis_index("half")
    z, x = lax.div(i, nx), lax.rem(i, nx)
    other_h = 1 - h
    x_next = nx - 1 - x

    barrier = pltpu.get_barrier_semaphore()

    def greet(t, _):
        pl.semaphore_signal(
            barrier, inc=1,
            device_id=(cut, lax.rem(i + lax.div(t, half), idx), lax.rem(h + lax.rem(t, half), half)),
            device_id_type=MESH,
        )
        return 0

    lax.fori_loop(1, group, greet, 0)
    pl.semaphore_wait(barrier, group - 1)

    upper = lax.div(z, nz // 2)
    from_end = z * (1 - upper) + (nz - 1 - z) * upper
    my_class = from_end
    per_class = 2 * nx * half

    def piece(j, cls, e):
        zb = lax.rem(upper + lax.div(e, half * nx), 2)
        to_z = cls + zb * (nz - 1 - 2 * cls)
        to_x = lax.rem(x + lax.rem(lax.div(e, half), nx), nx)
        to_h = lax.rem(h + lax.rem(e, half), half)
        to_i = to_z * nx + to_x
        return pltpu.make_async_remote_copy(
            src_ref=right_ref.at[:, (to_i * half + to_h) * mine + j],
            dst_ref=recv.at[j, h, :, pl.ds(i * rows, rows), :],
            send_sem=send_sem.at[j, cls * per_class + e],
            recv_sem=recv_sem.at[j, my_class * per_class + e],
            device_id=(cut, to_i, to_h), device_id_type=MESH,
        )

    def arrival(j, t):
        return pltpu.make_async_remote_copy(
            src_ref=right_ref.at[:, j], dst_ref=recv.at[j, h, :, pl.ds(i * rows, rows), :],
            send_sem=send_sem.at[j, t], recv_sem=recv_sem.at[j, t],
            device_id=(cut, i, other_h), device_id_type=MESH,
        )

    def own_piece(j):
        return pltpu.make_async_copy(
            right_ref.at[:, (i * half + h) * mine + j],
            recv.at[j, h, :, pl.ds(i * rows, rows), :], own_sem.at[j],
        )

    def start_group(cls, j):
        def go(k, _):
            e = lax.rem(k + my_class * half * nx + x * half + h, per_class)
            own = e + per_class * lax.rem(cls + my_class, 2)

            @pl.when(own != 0)
            def _():
                piece(j, cls, e).start()

            @pl.when(own == 0)
            def _():
                own_piece(j).start()

            return 0

        lax.fori_loop(0, per_class, go, 0)

    def others(step):
        def go(t, _):
            @pl.when(t != my_class * per_class)
            def _():
                step(t)
            return 0

        lax.fori_loop(0, group, go, 0)

    def wait_round(j):
        own_piece(j).wait()
        others(lambda t: arrival(j, t).wait_recv())

    def left_copy(j):
        return pltpu.make_async_remote_copy(
            src_ref=left_ref.at[:, other_h * mine + j], dst_ref=both_ref.at[h, j],
            send_sem=left_send.at[j], recv_sem=left_recv.at[j],
            device_id=(cut, i, other_h), device_id_type=MESH,
        )

    def left_keep(j):
        return pltpu.make_async_copy(left_ref.at[:, h * mine + j], both_ref.at[h, j], left_own.at[j])

    groups = sorted((12 * j + cls * (8 * j + 5), cls, j) for cls in range(2) for j in range(mine))
    for n, (_, cls, j) in enumerate(groups):
        start_group(cls, j)
        if n == 1:
            for k in range(mine):
                left_copy(k).start()
                left_keep(k).start()
    acc[...] = jnp.zeros_like(acc)

    def load_first(j, q):
        zz = lax.div(q, nx * half)
        xx = lax.rem(lax.div(q, half), nx)
        hh = lax.rem(q, half)
        to = ((hh * nx + xx) * nz + zz) * block
        return pltpu.make_async_copy(
            both_ref.at[0, j, :, pl.ds(q * block, block), :],
            a_buf.at[0, :, pl.ds(to, block), :], load_sem.at[q],
        )

    def load_second(j):
        return pltpu.make_async_copy(both_ref.at[1, j], a_buf.at[1], load_sem.at[group])

    def prepare(j):
        left_copy(j).wait_recv()
        left_keep(j).wait()

        def go(q, _):
            load_first(j, q).start()
            return 0

        def done(q, _):
            load_first(j, q).wait()
            return 0

        lax.fori_loop(0, group, go, 0)
        load_second(j).start()
        lax.fori_loop(0, group, done, 0)
        load_second(j).wait()

        def split(s, _):
            at = pl.ds(s * tile, tile)
            store_parts(a0, (at, slice(None)), a_buf[0, 0, at, :], a_buf[0, 1, at, :])
            store_parts(a1, (at, slice(None)), a_buf[1, 0, at, :], a_buf[1, 1, at, :])
            return 0

        lax.fori_loop(0, open_ // tile, split, 0)

    width = min(between, 256)

    def inner_product(j):
        c_acc[...] = jnp.zeros_like(c_acc)

        def go(s, _):
            at = pl.ds(pl.multiple_of(s * width, width), width)
            lr, li = recv[j, 0, 0, :, at], recv[j, 0, 1, :, at]
            rr, ri = recv[j, 1, 0, :, at], recv[j, 1, 1, :, at]
            c_acc[0] += product(parts_of(lr), parts_of(rr), NT)
            c_acc[1] += product(parts_of(li), parts_of(ri), NT)
            c_acc[2] += product(parts_of(lr + li), parts_of(rr + ri), NT)
            return 0

        lax.fori_loop(0, between // width, go, 0)
        real = c_acc[0] - c_acc[1]
        store_parts(c_parts, (), real, c_acc[2] - c_acc[0] - c_acc[1])

    def tile_product(t):
        at = pl.ds(pl.multiple_of(t * tile, tile), tile)
        first, second, mixed = (
            product((a0[p, 0, at, :], a0[p, 1, at, :]), (c_parts[p, 0], c_parts[p, 1]), NN)
            for p in range(3)
        )
        real, imag = first - second, mixed - first - second
        pr, pi, ps = parts_of(real), parts_of(imag), parts_of(real + imag)
        wide = min(open_, 1024)

        def go(s, _):
            o = pl.ds(pl.multiple_of(s * wide, wide), wide)
            t1, t2, t3 = (
                product(pp, (a1[p, 0, o, :], a1[p, 1, o, :]), NT)
                for p, pp in enumerate((pr, pi, ps))
            )
            acc[0, t, :, o] += t1 - t2
            acc[1, t, :, o] += t3 - t1 - t2
            return 0

        lax.fori_loop(0, open_ // wide, go, 0)

    for j in range(mine):
        prepare(j)
        wait_round(j)
        inner_product(j)
        if j < mine - 1:
            def all_tiles(t, _):
                tile_product(t)
                return 0

            lax.fori_loop(0, half * nx, all_tiles, 0)

    def core_copy(s, t):
        return pltpu.make_async_remote_copy(
            src_ref=acc.at[:, t], dst_ref=core_in.at[s],
            send_sem=core_send.at[s], recv_sem=core_recv.at[s],
            device_id=(cut, i, other_h), device_id_type=MESH,
        )

    away, here = h * nx + x_next, h * nx + x
    def place(s):
        p = nz - 1 - s if s < nz // 2 else lax.rem(from_end + nz - s - 1, nz // 2) if nz > 1 else 0
        return p * (1 - upper) + (nz - 1 - p) * upper

    def rows_of(zz):
        return pl.ds(pl.multiple_of(zz * block, block), block)

    def x_copy(s, p):
        return pltpu.make_async_remote_copy(
            src_ref=acc.at[p, away, rows_of(place(s)), :], dst_ref=x_in.at[s, p],
            send_sem=x_send.at[s, p], recv_sem=x_recv.at[s, p],
            device_id=(cut, z * nx + x_next, h), device_id_type=MESH,
        )

    def z_copy(way, zz, p):
        to_z = z + 1 - 2 * way
        return pltpu.make_async_remote_copy(
            src_ref=acc.at[p, here, rows_of(zz), :], dst_ref=z_in.at[way, zz, p],
            send_sem=z_send.at[way, zz, p], recv_sem=z_recv.at[way, zz, p],
            device_id=(cut, to_z * nx + x, h), device_id_type=MESH,
        )

    detour = DETOUR

    def detour_copy(s, p):
        k = detour.index((s, p))
        return pltpu.make_async_remote_copy(
            src_ref=acc.at[p, away, rows_of(place(s)), :], dst_ref=detour_in.at[k],
            send_sem=x_send.at[s, p], recv_sem=detour_recv.at[k],
            device_id=(cut, (z - 1 + 2 * upper) * nx + x_next, h), device_id_type=MESH,
        )

    def forward(s, p):
        k = detour.index((s, p))
        return pltpu.make_async_remote_copy(
            src_ref=detour_in.at[k], dst_ref=x_in.at[s, p],
            send_sem=detour_send.at[k], recv_sem=x_recv.at[s, p],
            device_id=(cut, (z + 1 - 2 * upper) * nx + x, h), device_id_type=MESH,
        )

    tile_product(other_h * nx + x_next)
    core_copy(0, other_h * nx + x_next).start()
    tile_product(away)
    core_copy(0, away).wait_recv()
    for s in range(nz):
        at = rows_of(place(s))
        for p in range(2):
            acc[p, away, at, :] += core_in[0, p, at, :]
            if (s, p) in detour:
                @pl.when(my_class != 0)
                def _():
                    detour_copy(s, p).start()

                @pl.when(my_class == 0)
                def _():
                    x_copy(s, p).start()
            else:
                x_copy(s, p).start()
    tile_product(other_h * nx + x)
    core_copy(1, other_h * nx + x).start()
    tile_product(here)
    core_copy(1, here).wait_recv()
    acc[:, here] += core_in[1]

    def pass_on(zz, p):
        at = rows_of(zz)

        @pl.when((zz >= z) & (z > 0))
        def _():
            z_copy(0, zz, p).wait_recv()
            acc[p, here, at, :] += z_in[0, zz, p]

        @pl.when((zz <= z) & (z < nz - 1))
        def _():
            z_copy(1, zz, p).wait_recv()
            acc[p, here, at, :] += z_in[1, zz, p]

        @pl.when(zz > z)
        def _():
            z_copy(0, zz, p).start()

        @pl.when(zz < z)
        def _():
            z_copy(1, zz, p).start()

    for s in range(nz):
        zz = place(s)
        at = rows_of(zz)
        if s == nz - 1:
            @pl.when(my_class == 0)
            def _():
                for step in detour:
                    detour_copy(*step).wait_recv()
                    forward(*step).start()
        for p in range(2):
            x_copy(s, p).wait_recv()
            acc[p, here, at, :] += x_in[s, p]
            pass_on(zz, p)
    for p in range(2):
        out_ref[:, p, :] = acc[p, here, rows_of(z), :] * norm_scale

    for s in range(nz):
        zz = place(s)
        for p in range(2):
            x_copy(s, p).wait_send()

            @pl.when(zz > z)
            def _():
                z_copy(0, zz, p).wait_send()

            @pl.when(zz < z)
            def _():
                z_copy(1, zz, p).wait_send()

    @pl.when(my_class == 0)
    def _():
        for step in detour:
            forward(*step).wait_send()

    core_copy(0, other_h * nx + x_next).wait_send()
    core_copy(1, other_h * nx + x).wait_send()
    for j in range(mine):
        left_copy(j).wait_send()
        others(lambda t: arrival(j, t).wait_send())


def by_kernel(left_local, right_local, norm_scale):
    idx, half = lax.axis_size("idx"), lax.axis_size("half")
    planes, per_idx, open_, inner = left_local.shape
    between = right_local.shape[3]
    mine = per_idx // half
    nx = 2
    nz = idx // nx
    group = idx * half
    block = open_ // group
    dma = pltpu.SemaphoreType.DMA
    sizes = (idx, half, mine, open_, inner, between, nx)
    complex_macs = mine * (inner * between * inner + open_ * inner * inner + open_ * inner * open_)
    out, _ = pl.pallas_call(
        functools.partial(kernel, sizes, norm_scale),
        out_shape=(
            jax.ShapeDtypeStruct((block, planes, open_), F32),
            jax.ShapeDtypeStruct((half, mine, planes, open_, inner), F32),
        ),
        in_specs=[pl.BlockSpec(memory_space=pl.ANY)] * 2,
        out_specs=(pl.BlockSpec(memory_space=pltpu.VMEM), pl.BlockSpec(memory_space=pl.ANY)),
        scratch_shapes=[
            pltpu.VMEM((mine, half, planes, inner, between), F32),
            pltpu.VMEM((half, planes, open_, inner), F32),
            pltpu.VMEM((3, 2, open_, inner), BF16),
            pltpu.VMEM((3, 2, open_, inner), BF16),
            pltpu.VMEM((3, inner, inner), F32),
            pltpu.VMEM((3, 2, inner, inner), BF16),
            pltpu.VMEM((planes, half * nx, nz * block, open_), F32),
            pltpu.VMEM((nx, planes, nz * block, open_), F32),
            pltpu.VMEM((nz, planes, block, open_), F32),
            pltpu.VMEM((2, nz, planes, block, open_), F32),
            pltpu.VMEM((len(DETOUR), block, open_), F32),
            dma((mine, group)), dma((mine, group)), dma((mine,)),
            dma((mine,)), dma((mine,)), dma((mine,)), dma((group + 1,)),
            dma((nx,)), dma((nx,)), dma((nz, planes)), dma((nz, planes)),
            dma((2, nz, planes)), dma((2, nz, planes)), dma((len(DETOUR),)), dma((len(DETOUR),)),
        ],
        compiler_params=pltpu.CompilerParams(
            collective_id=0, has_side_effects=True, vmem_limit_bytes=58 * 2**20
        ),
        cost_estimate=pl.CostEstimate(
            flops=18 * complex_macs, bytes_accessed=4 * (left_local.size + right_local.size), transcendentals=0
        ),
    )(left_local, right_local)
    return out


def swapped(x, axis, bit):
    return lax.ppermute(x, axis, [(i, i ^ 1 << bit) for i in range(lax.axis_size(axis))])


def complex_product(left_real, left_imag, right_real, right_imag, pattern):
    first_term = jnp.einsum(pattern, left_real, right_real, precision=HIGH)
    second_term = jnp.einsum(pattern, left_imag, right_imag, precision=HIGH)
    mixed_term = jnp.einsum(
        pattern, left_real + left_imag, right_real + right_imag, precision=HIGH
    )
    return (first_term - second_term, mixed_term - first_term - second_term)


def by_columns(left_local, right_local, norm_scale):
    columns = lax.all_to_all(right_local, "idx", split_axis=1, concat_axis=2, tiled=True)
    merged = jnp.stack(
        complex_product(left_local[0], left_local[1], columns[0], columns[1], "bmk,bkn->bmn")
    )
    half_cols = merged.shape[3] // 2
    half_index = lax.axis_index("half")
    outgoing = lax.dynamic_slice_in_dim(merged, (1 - half_index) * half_cols, half_cols, 3)
    own_slab = lax.dynamic_slice_in_dim(merged, half_index * half_cols, half_cols, 3)
    other_slab = swapped(outgoing, "half", 0)
    is_lower = half_index == 0
    first_pair = jnp.where(is_lower, own_slab, other_slab)
    second_pair = jnp.where(is_lower, other_slab, own_slab)
    real_part, imag_part = complex_product(
        first_pair[0], first_pair[1], second_pair[0], second_pair[1], "bmn,bon->mo"
    )
    return jnp.stack([real_part, imag_part], axis=1) * norm_scale


def on_device(left_factor, right_factor):
    left_local = left_factor[0]
    right_local = right_factor[0]
    batch, between = right_local.shape[1], right_local.shape[3]
    norm_scale = 1.0 / math.sqrt(2.0 * batch * between)
    idx, half = lax.axis_size("idx"), lax.axis_size("half")
    if half == 2 and idx == 2 * LINE and left_local.shape[1] % half == 0:
        return by_kernel(left_local, right_local, norm_scale)
    return lax.psum_scatter(
        by_columns(left_local, right_local, norm_scale),
        ("idx", "half"),
        scatter_dimension=0,
        tiled=True,
    )


def solution(mesh):
    return jax.shard_map(
        on_device,
        mesh=mesh,
        in_specs=(P("half", "cuts", "idx", None, None), P("half", "cuts", None, "idx", None)),
        out_specs=P(("idx", "half"), "cuts", None),
        check_vma=False,
    )
```

```python
import functools
import math

import jax
import jax.numpy as jnp
from jax import lax
from jax.experimental import pallas as pl
from jax.experimental.pallas import tpu as pltpu
from jax.sharding import PartitionSpec as P

HIGH = lax.Precision.HIGH
MESH = pl.DeviceIdType.MESH
F32 = jnp.float32
BF16 = jnp.bfloat16
NN = (((1,), (0,)), ((), ()))
LINE = 4
DETOUR = ((0, 1), (1, 1), (2, 1))
KEPT = ((2, 1),)
NT = (((1,), (1,)), ((), ()))


def parts_of(x):
    high = x.astype(BF16)
    return high, (x - high.astype(F32)).astype(BF16)


def product(left, right, dims):
    (xh, xl), (yh, yl) = left, right
    dot = functools.partial(lax.dot_general, dimension_numbers=dims, preferred_element_type=F32)
    return dot(xh, yh) + (dot(xh, yl) + dot(xl, yh))


def store_parts(ref, at, real, imag):
    for plane, x in enumerate((real, imag, real + imag)):
        high, low = parts_of(x)
        ref[(plane, 0) + at] = high
        ref[(plane, 1) + at] = low


def kernel(
    sizes, norm_scale,
    left_ref, right_ref, out_ref, both_ref,
    recv, a_buf, a0, a1, c_acc, c_parts, acc, core_in, x_in, z_in, detour_in,
    send_sem, recv_sem, own_sem, left_send, left_recv, left_own, load_sem,
    core_send, core_recv, x_send, x_recv, z_send, z_recv, detour_send, detour_recv, first_send, first_recv,
):
    idx, half, mine, open_, inner, between, nx = sizes
    nz = idx // nx
    block = open_ // (idx * half)
    tile = nz * block
    group = idx * half
    rows = inner // idx
    cut = lax.axis_index("cuts")
    i = lax.axis_index("idx")
    h = lax.axis_index("half")
    z, x = lax.div(i, nx), lax.rem(i, nx)
    other_h = 1 - h
    x_next = nx - 1 - x

    barrier = pltpu.get_barrier_semaphore()

    def greet(t, _):
        pl.semaphore_signal(
            barrier, inc=1,
            device_id=(cut, lax.rem(i + lax.div(t, half), idx), lax.rem(h + lax.rem(t, half), half)),
            device_id_type=MESH,
        )
        return 0

    lax.fori_loop(1, group, greet, 0)
    pl.semaphore_wait(barrier, group - 1)

    upper = lax.div(z, nz // 2)
    from_end = z * (1 - upper) + (nz - 1 - z) * upper
    my_class = from_end
    per_class = 2 * nx * half

    def piece(j, cls, e):
        zb = lax.rem(upper + lax.div(e, half * nx), 2)
        to_z = cls + zb * (nz - 1 - 2 * cls)
        to_x = lax.rem(x + lax.rem(lax.div(e, half), nx), nx)
        to_h = lax.rem(h + lax.rem(e, half), half)
        to_i = to_z * nx + to_x
        return pltpu.make_async_remote_copy(
            src_ref=right_ref.at[:, (to_i * half + to_h) * mine + j],
            dst_ref=recv.at[j, h, :, pl.ds(i * rows, rows), :],
            send_sem=send_sem.at[j, cls * per_class + e],
            recv_sem=recv_sem.at[j, my_class * per_class + e],
            device_id=(cut, to_i, to_h), device_id_type=MESH,
        )

    def arrival(j, t):
        return pltpu.make_async_remote_copy(
            src_ref=right_ref.at[:, j], dst_ref=recv.at[j, h, :, pl.ds(i * rows, rows), :],
            send_sem=send_sem.at[j, t], recv_sem=recv_sem.at[j, t],
            device_id=(cut, i, other_h), device_id_type=MESH,
        )

    def own_piece(j):
        return pltpu.make_async_copy(
            right_ref.at[:, (i * half + h) * mine + j],
            recv.at[j, h, :, pl.ds(i * rows, rows), :], own_sem.at[j],
        )

    def start_group(cls, j):
        def go(k, _):
            e = lax.rem(k + my_class * half * nx + upper * half + h, per_class)
            own = e + per_class * lax.rem(cls + my_class, 2)

            @pl.when(own != 0)
            def _():
                piece(j, cls, e).start()

            @pl.when(own == 0)
            def _():
                own_piece(j).start()

            return 0

        lax.fori_loop(0, per_class, go, 0)

    def others(step):
        def go(t, _):
            @pl.when(t != my_class * per_class)
            def _():
                step(t)
            return 0

        lax.fori_loop(0, group, go, 0)

    def wait_round(j):
        own_piece(j).wait()
        others(lambda t: arrival(j, t).wait_recv())

    def left_copy(j):
        return pltpu.make_async_remote_copy(
            src_ref=left_ref.at[:, other_h * mine + j], dst_ref=both_ref.at[h, j],
            send_sem=left_send.at[j], recv_sem=left_recv.at[j],
            device_id=(cut, i, other_h), device_id_type=MESH,
        )

    def left_keep(j):
        return pltpu.make_async_copy(left_ref.at[:, h * mine + j], both_ref.at[h, j], left_own.at[j])

    groups = sorted((12 * j + cls * (8 * j + 5), cls, j) for cls in range(2) for j in range(mine))
    for n, (_, cls, j) in enumerate(groups):
        start_group(cls, j)
        if n == 1:
            for k in range(mine):
                left_copy(k).start()
                left_keep(k).start()
    acc[...] = jnp.zeros_like(acc)

    def load_first(j, q):
        zz = lax.div(q, nx * half)
        xx = lax.rem(lax.div(q, half), nx)
        hh = lax.rem(q, half)
        to = ((hh * nx + xx) * nz + zz) * block
        return pltpu.make_async_copy(
            both_ref.at[0, j, :, pl.ds(q * block, block), :],
            a_buf.at[0, :, pl.ds(to, block), :], load_sem.at[q],
        )

    def load_second(j):
        return pltpu.make_async_copy(both_ref.at[1, j], a_buf.at[1], load_sem.at[group])

    def prepare(j):
        left_copy(j).wait_recv()
        left_keep(j).wait()

        def go(q, _):
            load_first(j, q).start()
            return 0

        def done(q, _):
            load_first(j, q).wait()
            return 0

        lax.fori_loop(0, group, go, 0)
        load_second(j).start()
        lax.fori_loop(0, group, done, 0)
        load_second(j).wait()

        def split(s, _):
            at = pl.ds(s * tile, tile)
            store_parts(a0, (at, slice(None)), a_buf[0, 0, at, :], a_buf[0, 1, at, :])
            store_parts(a1, (at, slice(None)), a_buf[1, 0, at, :], a_buf[1, 1, at, :])
            return 0

        lax.fori_loop(0, open_ // tile, split, 0)

    width = min(between, 256)

    def inner_product(j):
        c_acc[...] = jnp.zeros_like(c_acc)

        def go(s, _):
            at = pl.ds(pl.multiple_of(s * width, width), width)
            lr, li = recv[j, 0, 0, :, at], recv[j, 0, 1, :, at]
            rr, ri = recv[j, 1, 0, :, at], recv[j, 1, 1, :, at]
            c_acc[0] += product(parts_of(lr), parts_of(rr), NT)
            c_acc[1] += product(parts_of(li), parts_of(ri), NT)
            c_acc[2] += product(parts_of(lr + li), parts_of(rr + ri), NT)
            return 0

        lax.fori_loop(0, between // width, go, 0)
        real = c_acc[0] - c_acc[1]
        store_parts(c_parts, (), real, c_acc[2] - c_acc[0] - c_acc[1])

    def tile_product(t, start=0, count=tile):
        at = pl.ds(pl.multiple_of(t * tile + start, count), count)
        to = pl.ds(pl.multiple_of(start, count), count)
        first, second, mixed = (
            product((a0[p, 0, at, :], a0[p, 1, at, :]), (c_parts[p, 0], c_parts[p, 1]), NN)
            for p in range(3)
        )
        real, imag = first - second, mixed - first - second
        pr, pi, ps = parts_of(real), parts_of(imag), parts_of(real + imag)
        wide = min(open_, 1024)

        def go(s, _):
            o = pl.ds(pl.multiple_of(s * wide, wide), wide)
            t1, t2, t3 = (
                product(pp, (a1[p, 0, o, :], a1[p, 1, o, :]), NT)
                for p, pp in enumerate((pr, pi, ps))
            )
            acc[0, t, to, o] += t1 - t2
            acc[1, t, to, o] += t3 - t1 - t2
            return 0

        lax.fori_loop(0, open_ // wide, go, 0)

    for j in range(mine):
        prepare(j)
        wait_round(j)
        inner_product(j)
        if j < mine - 1:
            def all_tiles(t, _):
                tile_product(t)
                return 0

            lax.fori_loop(0, half * nx, all_tiles, 0)

    def core_copy(s, t):
        return pltpu.make_async_remote_copy(
            src_ref=acc.at[:, t], dst_ref=core_in.at[s],
            send_sem=core_send.at[s], recv_sem=core_recv.at[s],
            device_id=(cut, i, other_h), device_id_type=MESH,
        )

    away, here = h * nx + x_next, h * nx + x
    def place(s):
        p = nz - 1 - s if s < nz // 2 else lax.rem(from_end + nz - s - 1, nz // 2) if nz > 1 else 0
        return p * (1 - upper) + (nz - 1 - p) * upper

    def rows_of(zz):
        return pl.ds(pl.multiple_of(zz * block, block), block)

    def x_copy(s, p):
        return pltpu.make_async_remote_copy(
            src_ref=acc.at[p, away, rows_of(place(s)), :], dst_ref=x_in.at[s, p],
            send_sem=x_send.at[s, p], recv_sem=x_recv.at[s, p],
            device_id=(cut, z * nx + x_next, h), device_id_type=MESH,
        )

    def z_copy(way, zz, p):
        to_z = z + 1 - 2 * way
        return pltpu.make_async_remote_copy(
            src_ref=acc.at[p, here, rows_of(zz), :], dst_ref=z_in.at[way, zz, p],
            send_sem=z_send.at[way, zz, p], recv_sem=z_recv.at[way, zz, p],
            device_id=(cut, to_z * nx + x, h), device_id_type=MESH,
        )

    detour = DETOUR
    passed = [step for step in DETOUR if step not in KEPT]

    def detour_copy(s, p):
        k = detour.index((s, p))
        return pltpu.make_async_remote_copy(
            src_ref=acc.at[p, away, rows_of(place(s)), :], dst_ref=detour_in.at[k],
            send_sem=x_send.at[s, p], recv_sem=detour_recv.at[k],
            device_id=(cut, (z - 1 + 2 * upper) * nx + x_next, h), device_id_type=MESH,
        )

    def forward(s, p):
        k = detour.index((s, p))
        return pltpu.make_async_remote_copy(
            src_ref=detour_in.at[k], dst_ref=x_in.at[s, p],
            send_sem=detour_send.at[k], recv_sem=x_recv.at[s, p],
            device_id=(cut, (z + 1 - 2 * upper) * nx + x, h), device_id_type=MESH,
        )

    part = tile // 2
    there = other_h * nx + x_next

    def first_core(k):
        lo = pl.multiple_of((1 - upper) * (1 - k) * part + upper * k * part, part)
        return lo, pltpu.make_async_remote_copy(
            src_ref=acc.at[:, there, pl.ds(lo, part), :], dst_ref=core_in.at[0, :, pl.ds(lo, part), :],
            send_sem=first_send.at[k], recv_sem=first_recv.at[k],
            device_id=(cut, i, other_h), device_id_type=MESH,
        )

    for k in range(2):
        lo, copy = first_core(k)
        tile_product(there, lo, part)
        copy.start()
        tile_product(away, lo, part)
        copy.wait_recv()
        for s in range(k * nz // 2, (k + 1) * nz // 2):
            at = rows_of(place(s))
            for p in range(2):
                acc[p, away, at, :] += core_in[0, p, at, :]
                if (s, p) in detour:
                    @pl.when(my_class != 0)
                    def _():
                        detour_copy(s, p).start()

                    @pl.when(my_class == 0)
                    def _():
                        x_copy(s, p).start()
                else:
                    x_copy(s, p).start()
    tile_product(other_h * nx + x)
    core_copy(1, other_h * nx + x).start()
    tile_product(here)
    core_copy(1, here).wait_recv()
    acc[:, here] += core_in[1]

    def pass_on(zz, p):
        at = rows_of(zz)

        @pl.when((zz >= z) & (z > 0))
        def _():
            z_copy(0, zz, p).wait_recv()
            acc[p, here, at, :] += z_in[0, zz, p]

        @pl.when((zz <= z) & (z < nz - 1))
        def _():
            z_copy(1, zz, p).wait_recv()
            acc[p, here, at, :] += z_in[1, zz, p]

        @pl.when(zz > z)
        def _():
            z_copy(0, zz, p).start()

        @pl.when(zz < z)
        def _():
            z_copy(1, zz, p).start()

    for s in range(nz):
        zz = place(s)
        at = rows_of(zz)
        if s == nz - 1:
            @pl.when(my_class == 0)
            def _():
                for step in passed:
                    detour_copy(*step).wait_recv()
                    forward(*step).start()
                for step in KEPT:
                    detour_copy(*step).wait_recv()
                    acc[step[1], here, at, :] += detour_in[detour.index(step)]
        for p in range(2):
            def add_x():
                x_copy(s, p).wait_recv()
                acc[p, here, at, :] += x_in[s, p]

            if (s, p) in KEPT:
                pl.when(my_class == 0)(add_x)
            else:
                add_x()
            pass_on(zz, p)
    for p in range(2):
        out_ref[:, p, :] = acc[p, here, rows_of(z), :] * norm_scale

    for s in range(nz):
        zz = place(s)
        for p in range(2):
            x_copy(s, p).wait_send()

            @pl.when(zz > z)
            def _():
                z_copy(0, zz, p).wait_send()

            @pl.when(zz < z)
            def _():
                z_copy(1, zz, p).wait_send()

    @pl.when(my_class == 0)
    def _():
        for step in passed:
            forward(*step).wait_send()

    for k in range(2):
        first_core(k)[1].wait_send()
    core_copy(1, other_h * nx + x).wait_send()
    for j in range(mine):
        left_copy(j).wait_send()
        others(lambda t: arrival(j, t).wait_send())


def by_kernel(left_local, right_local, norm_scale):
    idx, half = lax.axis_size("idx"), lax.axis_size("half")
    planes, per_idx, open_, inner = left_local.shape
    between = right_local.shape[3]
    mine = per_idx // half
    nx = 2
    nz = idx // nx
    group = idx * half
    block = open_ // group
    dma = pltpu.SemaphoreType.DMA
    sizes = (idx, half, mine, open_, inner, between, nx)
    complex_macs = mine * (inner * between * inner + open_ * inner * inner + open_ * inner * open_)
    out, _ = pl.pallas_call(
        functools.partial(kernel, sizes, norm_scale),
        out_shape=(
            jax.ShapeDtypeStruct((block, planes, open_), F32),
            jax.ShapeDtypeStruct((half, mine, planes, open_, inner), F32),
        ),
        in_specs=[pl.BlockSpec(memory_space=pl.ANY)] * 2,
        out_specs=(pl.BlockSpec(memory_space=pltpu.VMEM), pl.BlockSpec(memory_space=pl.ANY)),
        scratch_shapes=[
            pltpu.VMEM((mine, half, planes, inner, between), F32),
            pltpu.VMEM((half, planes, open_, inner), F32),
            pltpu.VMEM((3, 2, open_, inner), BF16),
            pltpu.VMEM((3, 2, open_, inner), BF16),
            pltpu.VMEM((3, inner, inner), F32),
            pltpu.VMEM((3, 2, inner, inner), BF16),
            pltpu.VMEM((planes, half * nx, nz * block, open_), F32),
            pltpu.VMEM((nx, planes, nz * block, open_), F32),
            pltpu.VMEM((nz, planes, block, open_), F32),
            pltpu.VMEM((2, nz, planes, block, open_), F32),
            pltpu.VMEM((len(DETOUR), block, open_), F32),
            dma((mine, group)), dma((mine, group)), dma((mine,)),
            dma((mine,)), dma((mine,)), dma((mine,)), dma((group + 1,)),
            dma((nx,)), dma((nx,)), dma((nz, planes)), dma((nz, planes)),
            dma((2, nz, planes)), dma((2, nz, planes)), dma((len(DETOUR),)), dma((len(DETOUR),)),
            dma((2,)), dma((2,)),
        ],
        compiler_params=pltpu.CompilerParams(
            collective_id=0, has_side_effects=True, vmem_limit_bytes=58 * 2**20
        ),
        cost_estimate=pl.CostEstimate(
            flops=18 * complex_macs, bytes_accessed=4 * (left_local.size + right_local.size), transcendentals=0
        ),
    )(left_local, right_local)
    return out


def swapped(x, axis, bit):
    return lax.ppermute(x, axis, [(i, i ^ 1 << bit) for i in range(lax.axis_size(axis))])


def complex_product(left_real, left_imag, right_real, right_imag, pattern):
    first_term = jnp.einsum(pattern, left_real, right_real, precision=HIGH)
    second_term = jnp.einsum(pattern, left_imag, right_imag, precision=HIGH)
    mixed_term = jnp.einsum(
        pattern, left_real + left_imag, right_real + right_imag, precision=HIGH
    )
    return (first_term - second_term, mixed_term - first_term - second_term)


def by_columns(left_local, right_local, norm_scale):
    columns = lax.all_to_all(right_local, "idx", split_axis=1, concat_axis=2, tiled=True)
    merged = jnp.stack(
        complex_product(left_local[0], left_local[1], columns[0], columns[1], "bmk,bkn->bmn")
    )
    half_cols = merged.shape[3] // 2
    half_index = lax.axis_index("half")
    outgoing = lax.dynamic_slice_in_dim(merged, (1 - half_index) * half_cols, half_cols, 3)
    own_slab = lax.dynamic_slice_in_dim(merged, half_index * half_cols, half_cols, 3)
    other_slab = swapped(outgoing, "half", 0)
    is_lower = half_index == 0
    first_pair = jnp.where(is_lower, own_slab, other_slab)
    second_pair = jnp.where(is_lower, other_slab, own_slab)
    real_part, imag_part = complex_product(
        first_pair[0], first_pair[1], second_pair[0], second_pair[1], "bmn,bon->mo"
    )
    return jnp.stack([real_part, imag_part], axis=1) * norm_scale


def on_device(left_factor, right_factor):
    left_local = left_factor[0]
    right_local = right_factor[0]
    batch, between = right_local.shape[1], right_local.shape[3]
    norm_scale = 1.0 / math.sqrt(2.0 * batch * between)
    idx, half = lax.axis_size("idx"), lax.axis_size("half")
    if half == 2 and idx == 2 * LINE and left_local.shape[1] % half == 0:
        return by_kernel(left_local, right_local, norm_scale)
    return lax.psum_scatter(
        by_columns(left_local, right_local, norm_scale),
        ("idx", "half"),
        scatter_dimension=0,
        tiled=True,
    )


def solution(mesh):
    return jax.shard_map(
        on_device,
        mesh=mesh,
        in_specs=(P("half", "cuts", "idx", None, None), P("half", "cuts", None, "idx", None)),
        out_specs=P(("idx", "half"), "cuts", None),
        check_vma=False,
    )
```

```python
import functools
import math

import jax
import jax.numpy as jnp
from jax import lax
from jax.experimental import pallas as pl
from jax.experimental.pallas import tpu as pltpu
from jax.sharding import PartitionSpec as P

HIGH = lax.Precision.HIGH
MESH = pl.DeviceIdType.MESH
F32 = jnp.float32
BF16 = jnp.bfloat16
NN = (((1,), (0,)), ((), ()))
LINE = 4
DETOUR = ((0, 1), (1, 1), (2, 1))
KEPT = ((2, 1),)
NT = (((1,), (1,)), ((), ()))


def parts_of(x):
    high = x.astype(BF16)
    return high, (x - high.astype(F32)).astype(BF16)


def product(left, right, dims):
    (xh, xl), (yh, yl) = left, right
    dot = functools.partial(lax.dot_general, dimension_numbers=dims, preferred_element_type=F32)
    return dot(xh, yh) + (dot(xh, yl) + dot(xl, yh))


def store_parts(ref, at, real, imag):
    for plane, x in enumerate((real, imag, real + imag)):
        high, low = parts_of(x)
        ref[(plane, 0) + at] = high
        ref[(plane, 1) + at] = low


def kernel(
    sizes, norm_scale,
    left_ref, right_ref, out_ref, both_ref,
    recv, a_buf, a0, a1, c_acc, c_parts, acc, core_in, x_in, z_in, detour_in,
    send_sem, recv_sem, own_sem, left_send, left_recv, left_own, load_sem,
    core_send, core_recv, x_send, x_recv, z_send, z_recv, detour_send, detour_recv,
):
    idx, half, mine, open_, inner, between, nx = sizes
    nz = idx // nx
    block = open_ // (idx * half)
    tile = nz * block
    group = idx * half
    rows = inner // idx
    cut = lax.axis_index("cuts")
    i = lax.axis_index("idx")
    h = lax.axis_index("half")
    z, x = lax.div(i, nx), lax.rem(i, nx)
    other_h = 1 - h
    x_next = nx - 1 - x

    barrier = pltpu.get_barrier_semaphore()

    def greet(t, _):
        pl.semaphore_signal(
            barrier, inc=1,
            device_id=(cut, lax.rem(i + lax.div(t, half), idx), lax.rem(h + lax.rem(t, half), half)),
            device_id_type=MESH,
        )
        return 0

    lax.fori_loop(1, group, greet, 0)
    pl.semaphore_wait(barrier, group - 1)

    upper = lax.div(z, nz // 2)
    from_end = z * (1 - upper) + (nz - 1 - z) * upper
    my_class = from_end
    per_class = 2 * nx * half

    def piece(j, cls, e):
        zb = lax.rem(upper + lax.div(e, half * nx), 2)
        to_z = cls + zb * (nz - 1 - 2 * cls)
        to_x = lax.rem(x + lax.rem(lax.div(e, half), nx), nx)
        to_h = lax.rem(h + lax.rem(e, half), half)
        to_i = to_z * nx + to_x
        return pltpu.make_async_remote_copy(
            src_ref=right_ref.at[:, (to_i * half + to_h) * mine + j],
            dst_ref=recv.at[j, h, :, pl.ds(i * rows, rows), :],
            send_sem=send_sem.at[j, cls * per_class + e],
            recv_sem=recv_sem.at[j, my_class * per_class + e],
            device_id=(cut, to_i, to_h), device_id_type=MESH,
        )

    def arrival(j, t):
        return pltpu.make_async_remote_copy(
            src_ref=right_ref.at[:, j], dst_ref=recv.at[j, h, :, pl.ds(i * rows, rows), :],
            send_sem=send_sem.at[j, t], recv_sem=recv_sem.at[j, t],
            device_id=(cut, i, other_h), device_id_type=MESH,
        )

    def own_piece(j):
        return pltpu.make_async_copy(
            right_ref.at[:, (i * half + h) * mine + j],
            recv.at[j, h, :, pl.ds(i * rows, rows), :], own_sem.at[j],
        )

    def start_group(cls, j):
        def go(k, _):
            e = lax.rem(k + my_class * half * nx + upper * half + h, per_class)
            own = e + per_class * lax.rem(cls + my_class, 2)

            @pl.when(own != 0)
            def _():
                piece(j, cls, e).start()

            @pl.when(own == 0)
            def _():
                own_piece(j).start()

            return 0

        lax.fori_loop(0, per_class, go, 0)

    def others(step):
        def go(t, _):
            @pl.when(t != my_class * per_class)
            def _():
                step(t)
            return 0

        lax.fori_loop(0, group, go, 0)

    def wait_round(j):
        own_piece(j).wait()
        others(lambda t: arrival(j, t).wait_recv())

    def left_copy(j):
        return pltpu.make_async_remote_copy(
            src_ref=left_ref.at[:, other_h * mine + j], dst_ref=both_ref.at[h, j],
            send_sem=left_send.at[j], recv_sem=left_recv.at[j],
            device_id=(cut, i, other_h), device_id_type=MESH,
        )

    def left_keep(j):
        return pltpu.make_async_copy(left_ref.at[:, h * mine + j], both_ref.at[h, j], left_own.at[j])

    groups = sorted((12 * j + cls * (8 * j + 5), cls, j) for cls in range(2) for j in range(mine))
    for n, (_, cls, j) in enumerate(groups):
        start_group(cls, j)
        if n == 1:
            for k in range(mine):
                left_copy(k).start()
                left_keep(k).start()
    acc[...] = jnp.zeros_like(acc)

    def load_first(j, q):
        zz = lax.div(q, nx * half)
        xx = lax.rem(lax.div(q, half), nx)
        hh = lax.rem(q, half)
        to = ((hh * nx + xx) * nz + zz) * block
        return pltpu.make_async_copy(
            both_ref.at[0, j, :, pl.ds(q * block, block), :],
            a_buf.at[0, :, pl.ds(to, block), :], load_sem.at[q],
        )

    def load_second(j):
        return pltpu.make_async_copy(both_ref.at[1, j], a_buf.at[1], load_sem.at[group])

    def prepare(j):
        left_copy(j).wait_recv()
        left_keep(j).wait()

        def go(q, _):
            load_first(j, q).start()
            return 0

        def done(q, _):
            load_first(j, q).wait()
            return 0

        lax.fori_loop(0, group, go, 0)
        load_second(j).start()
        lax.fori_loop(0, group, done, 0)
        load_second(j).wait()

        def split(s, _):
            at = pl.ds(s * tile, tile)
            store_parts(a0, (at, slice(None)), a_buf[0, 0, at, :], a_buf[0, 1, at, :])
            store_parts(a1, (at, slice(None)), a_buf[1, 0, at, :], a_buf[1, 1, at, :])
            return 0

        lax.fori_loop(0, open_ // tile, split, 0)

    width = min(between, 256)

    def inner_product(j):
        c_acc[...] = jnp.zeros_like(c_acc)

        def go(s, _):
            at = pl.ds(pl.multiple_of(s * width, width), width)
            lr, li = recv[j, 0, 0, :, at], recv[j, 0, 1, :, at]
            rr, ri = recv[j, 1, 0, :, at], recv[j, 1, 1, :, at]
            c_acc[0] += product(parts_of(lr), parts_of(rr), NT)
            c_acc[1] += product(parts_of(li), parts_of(ri), NT)
            c_acc[2] += product(parts_of(lr + li), parts_of(rr + ri), NT)
            return 0

        lax.fori_loop(0, between // width, go, 0)
        real = c_acc[0] - c_acc[1]
        store_parts(c_parts, (), real, c_acc[2] - c_acc[0] - c_acc[1])

    def tile_product(t, start=0, count=tile):
        at = pl.ds(pl.multiple_of(t * tile + start, count), count)
        to = pl.ds(pl.multiple_of(start, count), count)
        first, second, mixed = (
            product((a0[p, 0, at, :], a0[p, 1, at, :]), (c_parts[p, 0], c_parts[p, 1]), NN)
            for p in range(3)
        )
        real, imag = first - second, mixed - first - second
        pr, pi, ps = parts_of(real), parts_of(imag), parts_of(real + imag)
        wide = min(open_, 1024)

        def go(s, _):
            o = pl.ds(pl.multiple_of(s * wide, wide), wide)
            t1, t2, t3 = (
                product(pp, (a1[p, 0, o, :], a1[p, 1, o, :]), NT)
                for p, pp in enumerate((pr, pi, ps))
            )
            acc[0, t, to, o] += t1 - t2
            acc[1, t, to, o] += t3 - t1 - t2
            return 0

        lax.fori_loop(0, open_ // wide, go, 0)

    for j in range(mine):
        prepare(j)
        wait_round(j)
        inner_product(j)
        if j < mine - 1:
            def all_tiles(t, _):
                tile_product(t)
                return 0

            lax.fori_loop(0, half * nx, all_tiles, 0)

    away, here = h * nx + x_next, h * nx + x
    def place(s):
        p = nz - 1 - s if s < nz // 2 else lax.rem(from_end + nz - s - 1, nz // 2) if nz > 1 else 0
        return p * (1 - upper) + (nz - 1 - p) * upper

    def rows_of(zz):
        return pl.ds(pl.multiple_of(zz * block, block), block)

    def x_copy(s, p):
        return pltpu.make_async_remote_copy(
            src_ref=acc.at[p, away, rows_of(place(s)), :], dst_ref=x_in.at[s, p],
            send_sem=x_send.at[s, p], recv_sem=x_recv.at[s, p],
            device_id=(cut, z * nx + x_next, h), device_id_type=MESH,
        )

    def z_copy(way, zz, p):
        to_z = z + 1 - 2 * way
        return pltpu.make_async_remote_copy(
            src_ref=acc.at[p, here, rows_of(zz), :], dst_ref=z_in.at[way, zz, p],
            send_sem=z_send.at[way, zz, p], recv_sem=z_recv.at[way, zz, p],
            device_id=(cut, to_z * nx + x, h), device_id_type=MESH,
        )

    detour = DETOUR
    passed = [step for step in DETOUR if step not in KEPT]

    def detour_copy(s, p):
        k = detour.index((s, p))
        return pltpu.make_async_remote_copy(
            src_ref=acc.at[p, away, rows_of(place(s)), :], dst_ref=detour_in.at[k],
            send_sem=x_send.at[s, p], recv_sem=detour_recv.at[k],
            device_id=(cut, (z - 1 + 2 * upper) * nx + x_next, h), device_id_type=MESH,
        )

    def forward(s, p):
        k = detour.index((s, p))
        return pltpu.make_async_remote_copy(
            src_ref=detour_in.at[k], dst_ref=x_in.at[s, p],
            send_sem=detour_send.at[k], recv_sem=x_recv.at[s, p],
            device_id=(cut, (z + 1 - 2 * upper) * nx + x, h), device_id_type=MESH,
        )

    part = tile // 2
    tiles = (other_h * nx + x_next, other_h * nx + x)

    def low(k):
        return pl.multiple_of((1 - upper) * (1 - k) * part + upper * k * part, part)

    def core_copy(n, k):
        at = pl.ds(low(k), part)
        return pltpu.make_async_remote_copy(
            src_ref=acc.at[:, tiles[n], at, :], dst_ref=core_in.at[n, :, at, :],
            send_sem=core_send.at[n, k], recv_sem=core_recv.at[n, k],
            device_id=(cut, i, other_h), device_id_type=MESH,
        )

    def away_half(k):
        tile_product(tiles[0], low(k), part)
        core_copy(0, k).start()
        tile_product(away, low(k), part)
        core_copy(0, k).wait_recv()
        for s in range(k * nz // 2, (k + 1) * nz // 2):
            at = rows_of(place(s))
            for p in range(2):
                acc[p, away, at, :] += core_in[0, p, at, :]
                if (s, p) in detour:
                    @pl.when(my_class != 0)
                    def _():
                        detour_copy(s, p).start()

                    @pl.when(my_class == 0)
                    def _():
                        x_copy(s, p).start()
                else:
                    x_copy(s, p).start()

    def here_half(k):
        tile_product(tiles[1], low(k), part)
        core_copy(1, k).start()
        tile_product(here, low(k), part)
        core_copy(1, k).wait_recv()
        at = pl.ds(low(k), part)
        acc[:, here, at, :] += core_in[1, :, at, :]

    def pass_on(zz, p):
        at = rows_of(zz)

        @pl.when((zz >= z) & (z > 0))
        def _():
            z_copy(0, zz, p).wait_recv()
            acc[p, here, at, :] += z_in[0, zz, p]

        @pl.when((zz <= z) & (z < nz - 1))
        def _():
            z_copy(1, zz, p).wait_recv()
            acc[p, here, at, :] += z_in[1, zz, p]

        @pl.when(zz > z)
        def _():
            z_copy(0, zz, p).start()

        @pl.when(zz < z)
        def _():
            z_copy(1, zz, p).start()

    def settle(s, p):
        zz = place(s)

        def add_x():
            x_copy(s, p).wait_recv()
            acc[p, here, rows_of(zz), :] += x_in[s, p]

        if (s, p) in KEPT:
            pl.when(my_class == 0)(add_x)
        else:
            add_x()
        pass_on(zz, p)

    away_half(0)
    here_half(0)
    away_half(1)
    settle(0, 0)
    here_half(1)
    for s in range(nz):
        if s == nz - 1:
            @pl.when(my_class == 0)
            def _():
                for step in passed:
                    detour_copy(*step).wait_recv()
                    forward(*step).start()
                for step in KEPT:
                    detour_copy(*step).wait_recv()
                    acc[step[1], here, rows_of(place(s)), :] += detour_in[detour.index(step)]
        for p in range(2):
            if (s, p) != (0, 0):
                settle(s, p)
    for p in range(2):
        out_ref[:, p, :] = acc[p, here, rows_of(z), :] * norm_scale

    for s in range(nz):
        zz = place(s)
        for p in range(2):
            x_copy(s, p).wait_send()

            @pl.when(zz > z)
            def _():
                z_copy(0, zz, p).wait_send()

            @pl.when(zz < z)
            def _():
                z_copy(1, zz, p).wait_send()

    @pl.when(my_class == 0)
    def _():
        for step in passed:
            forward(*step).wait_send()

    for n in range(2):
        for k in range(2):
            core_copy(n, k).wait_send()
    for j in range(mine):
        left_copy(j).wait_send()
        others(lambda t: arrival(j, t).wait_send())


def by_kernel(left_local, right_local, norm_scale):
    idx, half = lax.axis_size("idx"), lax.axis_size("half")
    planes, per_idx, open_, inner = left_local.shape
    between = right_local.shape[3]
    mine = per_idx // half
    nx = 2
    nz = idx // nx
    group = idx * half
    block = open_ // group
    dma = pltpu.SemaphoreType.DMA
    sizes = (idx, half, mine, open_, inner, between, nx)
    complex_macs = mine * (inner * between * inner + open_ * inner * inner + open_ * inner * open_)
    out, _ = pl.pallas_call(
        functools.partial(kernel, sizes, norm_scale),
        out_shape=(
            jax.ShapeDtypeStruct((block, planes, open_), F32),
            jax.ShapeDtypeStruct((half, mine, planes, open_, inner), F32),
        ),
        in_specs=[pl.BlockSpec(memory_space=pl.ANY)] * 2,
        out_specs=(pl.BlockSpec(memory_space=pltpu.VMEM), pl.BlockSpec(memory_space=pl.ANY)),
        scratch_shapes=[
            pltpu.VMEM((mine, half, planes, inner, between), F32),
            pltpu.VMEM((half, planes, open_, inner), F32),
            pltpu.VMEM((3, 2, open_, inner), BF16),
            pltpu.VMEM((3, 2, open_, inner), BF16),
            pltpu.VMEM((3, inner, inner), F32),
            pltpu.VMEM((3, 2, inner, inner), BF16),
            pltpu.VMEM((planes, half * nx, nz * block, open_), F32),
            pltpu.VMEM((nx, planes, nz * block, open_), F32),
            pltpu.VMEM((nz, planes, block, open_), F32),
            pltpu.VMEM((2, nz, planes, block, open_), F32),
            pltpu.VMEM((len(DETOUR), block, open_), F32),
            dma((mine, group)), dma((mine, group)), dma((mine,)),
            dma((mine,)), dma((mine,)), dma((mine,)), dma((group + 1,)),
            dma((nx, 2)), dma((nx, 2)), dma((nz, planes)), dma((nz, planes)),
            dma((2, nz, planes)), dma((2, nz, planes)), dma((len(DETOUR),)), dma((len(DETOUR),)),
        ],
        compiler_params=pltpu.CompilerParams(
            collective_id=0, has_side_effects=True, vmem_limit_bytes=58 * 2**20
        ),
        cost_estimate=pl.CostEstimate(
            flops=18 * complex_macs, bytes_accessed=4 * (left_local.size + right_local.size), transcendentals=0
        ),
    )(left_local, right_local)
    return out


def swapped(x, axis, bit):
    return lax.ppermute(x, axis, [(i, i ^ 1 << bit) for i in range(lax.axis_size(axis))])


def complex_product(left_real, left_imag, right_real, right_imag, pattern):
    first_term = jnp.einsum(pattern, left_real, right_real, precision=HIGH)
    second_term = jnp.einsum(pattern, left_imag, right_imag, precision=HIGH)
    mixed_term = jnp.einsum(
        pattern, left_real + left_imag, right_real + right_imag, precision=HIGH
    )
    return (first_term - second_term, mixed_term - first_term - second_term)


def by_columns(left_local, right_local, norm_scale):
    columns = lax.all_to_all(right_local, "idx", split_axis=1, concat_axis=2, tiled=True)
    merged = jnp.stack(
        complex_product(left_local[0], left_local[1], columns[0], columns[1], "bmk,bkn->bmn")
    )
    half_cols = merged.shape[3] // 2
    half_index = lax.axis_index("half")
    outgoing = lax.dynamic_slice_in_dim(merged, (1 - half_index) * half_cols, half_cols, 3)
    own_slab = lax.dynamic_slice_in_dim(merged, half_index * half_cols, half_cols, 3)
    other_slab = swapped(outgoing, "half", 0)
    is_lower = half_index == 0
    first_pair = jnp.where(is_lower, own_slab, other_slab)
    second_pair = jnp.where(is_lower, other_slab, own_slab)
    real_part, imag_part = complex_product(
        first_pair[0], first_pair[1], second_pair[0], second_pair[1], "bmn,bon->mo"
    )
    return jnp.stack([real_part, imag_part], axis=1) * norm_scale


def on_device(left_factor, right_factor):
    left_local = left_factor[0]
    right_local = right_factor[0]
    batch, between = right_local.shape[1], right_local.shape[3]
    norm_scale = 1.0 / math.sqrt(2.0 * batch * between)
    idx, half = lax.axis_size("idx"), lax.axis_size("half")
    if half == 2 and idx == 2 * LINE and left_local.shape[1] % half == 0:
        return by_kernel(left_local, right_local, norm_scale)
    return lax.psum_scatter(
        by_columns(left_local, right_local, norm_scale),
        ("idx", "half"),
        scatter_dimension=0,
        tiled=True,
    )


def solution(mesh):
    return jax.shard_map(
        on_device,
        mesh=mesh,
        in_specs=(P("half", "cuts", "idx", None, None), P("half", "cuts", None, "idx", None)),
        out_specs=P(("idx", "half"), "cuts", None),
        check_vma=False,
    )
```

```python
import functools
import math

import jax
import jax.numpy as jnp
from jax import lax
from jax.experimental import pallas as pl
from jax.experimental.pallas import tpu as pltpu
from jax.sharding import PartitionSpec as P

HIGH = lax.Precision.HIGH
MESH = pl.DeviceIdType.MESH
F32 = jnp.float32
BF16 = jnp.bfloat16
NN = (((1,), (0,)), ((), ()))
LINE = 4
DETOUR = ((0, 1), (1, 1), (2, 1))
KEPT = ((2, 1),)
NT = (((1,), (1,)), ((), ()))


def parts_of(x):
    high = x.astype(BF16)
    return high, (x - high.astype(F32)).astype(BF16)


def product(left, right, dims):
    (xh, xl), (yh, yl) = left, right
    dot = functools.partial(lax.dot_general, dimension_numbers=dims, preferred_element_type=F32)
    return dot(xh, yh) + (dot(xh, yl) + dot(xl, yh))


def store_parts(ref, at, real, imag):
    for plane, x in enumerate((real, imag, real + imag)):
        high, low = parts_of(x)
        ref[(plane, 0) + at] = high
        ref[(plane, 1) + at] = low


def kernel(
    sizes, norm_scale,
    left_ref, right_ref, out_ref, both_ref,
    recv, a_buf, a0, a1, c_acc, c_parts, acc, core_in, x_in, z_in, detour_in,
    send_sem, recv_sem, own_sem, left_send, left_recv, left_own, load_sem,
    core_send, core_recv, x_send, x_recv, z_send, z_recv, detour_send, detour_recv,
):
    idx, half, mine, open_, inner, between, nx = sizes
    nz = idx // nx
    block = open_ // (idx * half)
    tile = nz * block
    group = idx * half
    rows = inner // idx
    cut = lax.axis_index("cuts")
    i = lax.axis_index("idx")
    h = lax.axis_index("half")
    z, x = lax.div(i, nx), lax.rem(i, nx)
    other_h = 1 - h
    x_next = nx - 1 - x

    barrier = pltpu.get_barrier_semaphore()

    def greet(t, _):
        pl.semaphore_signal(
            barrier, inc=1,
            device_id=(cut, lax.rem(i + lax.div(t, half), idx), lax.rem(h + lax.rem(t, half), half)),
            device_id_type=MESH,
        )
        return 0

    lax.fori_loop(1, group, greet, 0)
    pl.semaphore_wait(barrier, group - 1)

    upper = lax.div(z, nz // 2)
    from_end = z * (1 - upper) + (nz - 1 - z) * upper
    my_class = from_end
    per_class = 2 * nx * half

    def piece(j, cls, e):
        zb = lax.rem(upper + lax.div(e, half * nx), 2)
        to_z = cls + zb * (nz - 1 - 2 * cls)
        to_x = lax.rem(x + lax.rem(lax.div(e, half), nx), nx)
        to_h = lax.rem(h + lax.rem(e, half), half)
        to_i = to_z * nx + to_x
        return pltpu.make_async_remote_copy(
            src_ref=right_ref.at[:, (to_i * half + to_h) * mine + j],
            dst_ref=recv.at[j, h, :, pl.ds(i * rows, rows), :],
            send_sem=send_sem.at[j, cls * per_class + e],
            recv_sem=recv_sem.at[j, my_class * per_class + e],
            device_id=(cut, to_i, to_h), device_id_type=MESH,
        )

    def arrival(j, t):
        return pltpu.make_async_remote_copy(
            src_ref=right_ref.at[:, j], dst_ref=recv.at[j, h, :, pl.ds(i * rows, rows), :],
            send_sem=send_sem.at[j, t], recv_sem=recv_sem.at[j, t],
            device_id=(cut, i, other_h), device_id_type=MESH,
        )

    def own_piece(j):
        return pltpu.make_async_copy(
            right_ref.at[:, (i * half + h) * mine + j],
            recv.at[j, h, :, pl.ds(i * rows, rows), :], own_sem.at[j],
        )

    def start_group(cls, j):
        def go(k, _):
            e = lax.rem(k + my_class * half * nx + upper * half + h, per_class)
            own = e + per_class * lax.rem(cls + my_class, 2)

            @pl.when(own != 0)
            def _():
                piece(j, cls, e).start()

            @pl.when(own == 0)
            def _():
                own_piece(j).start()

            return 0

        lax.fori_loop(0, per_class, go, 0)

    def others(step):
        def go(t, _):
            @pl.when(t != my_class * per_class)
            def _():
                step(t)
            return 0

        lax.fori_loop(0, group, go, 0)

    def wait_round(j):
        own_piece(j).wait()
        others(lambda t: arrival(j, t).wait_recv())

    def left_copy(j):
        return pltpu.make_async_remote_copy(
            src_ref=left_ref.at[:, other_h * mine + j], dst_ref=both_ref.at[h, j],
            send_sem=left_send.at[j], recv_sem=left_recv.at[j],
            device_id=(cut, i, other_h), device_id_type=MESH,
        )

    def left_keep(j):
        return pltpu.make_async_copy(left_ref.at[:, h * mine + j], both_ref.at[h, j], left_own.at[j])

    groups = sorted((12 * j + cls * (8 * j + 5), cls, j) for cls in range(2) for j in range(mine))
    for n, (_, cls, j) in enumerate(groups):
        start_group(cls, j)
        if n == 1:
            for k in range(mine):
                left_copy(k).start()
                left_keep(k).start()
    acc[...] = jnp.zeros_like(acc)

    def load_first(j, q):
        zz = lax.div(q, nx * half)
        xx = lax.rem(lax.div(q, half), nx)
        hh = lax.rem(q, half)
        to = ((hh * nx + xx) * nz + zz) * block
        return pltpu.make_async_copy(
            both_ref.at[0, j, :, pl.ds(q * block, block), :],
            a_buf.at[0, :, pl.ds(to, block), :], load_sem.at[q],
        )

    def load_second(j):
        return pltpu.make_async_copy(both_ref.at[1, j], a_buf.at[1], load_sem.at[group])

    def prepare(j):
        left_copy(j).wait_recv()
        left_keep(j).wait()

        def go(q, _):
            load_first(j, q).start()
            return 0

        def done(q, _):
            load_first(j, q).wait()
            return 0

        lax.fori_loop(0, group, go, 0)
        load_second(j).start()
        lax.fori_loop(0, group, done, 0)
        load_second(j).wait()

        def split(s, _):
            at = pl.ds(s * tile, tile)
            store_parts(a0, (at, slice(None)), a_buf[0, 0, at, :], a_buf[0, 1, at, :])
            store_parts(a1, (at, slice(None)), a_buf[1, 0, at, :], a_buf[1, 1, at, :])
            return 0

        lax.fori_loop(0, open_ // tile, split, 0)

    width = min(between, 1024)

    def inner_product(j):
        c_acc[...] = jnp.zeros_like(c_acc)

        def go(s, _):
            at = pl.ds(pl.multiple_of(s * width, width), width)
            lr, li = recv[j, 0, 0, :, at], recv[j, 0, 1, :, at]
            rr, ri = recv[j, 1, 0, :, at], recv[j, 1, 1, :, at]
            c_acc[0] += product(parts_of(lr), parts_of(rr), NT)
            c_acc[1] += product(parts_of(li), parts_of(ri), NT)
            c_acc[2] += product(parts_of(lr + li), parts_of(rr + ri), NT)
            return 0

        lax.fori_loop(0, between // width, go, 0)
        real = c_acc[0] - c_acc[1]
        store_parts(c_parts, (), real, c_acc[2] - c_acc[0] - c_acc[1])

    def tile_product(t, start=0, count=tile):
        at = pl.ds(pl.multiple_of(t * tile + start, count), count)
        to = pl.ds(pl.multiple_of(start, count), count)
        first, second, mixed = (
            product((a0[p, 0, at, :], a0[p, 1, at, :]), (c_parts[p, 0], c_parts[p, 1]), NN)
            for p in range(3)
        )
        real, imag = first - second, mixed - first - second
        pr, pi, ps = parts_of(real), parts_of(imag), parts_of(real + imag)
        wide = min(open_, 1024)

        def go(s, _):
            o = pl.ds(pl.multiple_of(s * wide, wide), wide)
            t1, t2, t3 = (
                product(pp, (a1[p, 0, o, :], a1[p, 1, o, :]), NT)
                for p, pp in enumerate((pr, pi, ps))
            )
            acc[0, t, to, o] += t1 - t2
            acc[1, t, to, o] += t3 - t1 - t2
            return 0

        lax.fori_loop(0, open_ // wide, go, 0)

    for j in range(mine):
        prepare(j)
        wait_round(j)
        inner_product(j)
        if j < mine - 1:
            def all_tiles(t, _):
                tile_product(t)
                return 0

            lax.fori_loop(0, half * nx, all_tiles, 0)

    away, here = h * nx + x_next, h * nx + x
    def place(s):
        p = nz - 1 - s if s < nz // 2 else lax.rem(from_end + nz - s - 1, nz // 2) if nz > 1 else 0
        return p * (1 - upper) + (nz - 1 - p) * upper

    def rows_of(zz):
        return pl.ds(pl.multiple_of(zz * block, block), block)

    def x_copy(s, p):
        return pltpu.make_async_remote_copy(
            src_ref=acc.at[p, away, rows_of(place(s)), :], dst_ref=x_in.at[s, p],
            send_sem=x_send.at[s, p], recv_sem=x_recv.at[s, p],
            device_id=(cut, z * nx + x_next, h), device_id_type=MESH,
        )

    def z_copy(way, zz, p):
        to_z = z + 1 - 2 * way
        return pltpu.make_async_remote_copy(
            src_ref=acc.at[p, here, rows_of(zz), :], dst_ref=z_in.at[way, zz, p],
            send_sem=z_send.at[way, zz, p], recv_sem=z_recv.at[way, zz, p],
            device_id=(cut, to_z * nx + x, h), device_id_type=MESH,
        )

    detour = DETOUR
    passed = [step for step in DETOUR if step not in KEPT]

    def detour_copy(s, p):
        k = detour.index((s, p))
        return pltpu.make_async_remote_copy(
            src_ref=acc.at[p, away, rows_of(place(s)), :], dst_ref=detour_in.at[k],
            send_sem=x_send.at[s, p], recv_sem=detour_recv.at[k],
            device_id=(cut, (z - 1 + 2 * upper) * nx + x_next, h), device_id_type=MESH,
        )

    def forward(s, p):
        k = detour.index((s, p))
        return pltpu.make_async_remote_copy(
            src_ref=detour_in.at[k], dst_ref=x_in.at[s, p],
            send_sem=detour_send.at[k], recv_sem=x_recv.at[s, p],
            device_id=(cut, (z + 1 - 2 * upper) * nx + x, h), device_id_type=MESH,
        )

    part = tile // 2
    tiles = (other_h * nx + x_next, other_h * nx + x)

    def low(k):
        return pl.multiple_of((1 - upper) * (1 - k) * part + upper * k * part, part)

    def core_copy(n, k):
        at = pl.ds(low(k), part)
        return pltpu.make_async_remote_copy(
            src_ref=acc.at[:, tiles[n], at, :], dst_ref=core_in.at[n, :, at, :],
            send_sem=core_send.at[n, k], recv_sem=core_recv.at[n, k],
            device_id=(cut, i, other_h), device_id_type=MESH,
        )

    def away_half(k):
        tile_product(tiles[0], low(k), part)
        core_copy(0, k).start()
        tile_product(away, low(k), part)
        core_copy(0, k).wait_recv()
        for s in range(k * nz // 2, (k + 1) * nz // 2):
            at = rows_of(place(s))
            for p in range(2):
                acc[p, away, at, :] += core_in[0, p, at, :]
                if (s, p) in detour:
                    @pl.when(my_class != 0)
                    def _():
                        detour_copy(s, p).start()

                    @pl.when(my_class == 0)
                    def _():
                        x_copy(s, p).start()
                else:
                    x_copy(s, p).start()

    def here_half(k):
        tile_product(tiles[1], low(k), part)
        core_copy(1, k).start()
        tile_product(here, low(k), part)
        core_copy(1, k).wait_recv()
        at = pl.ds(low(k), part)
        acc[:, here, at, :] += core_in[1, :, at, :]

    def pass_on(zz, p):
        at = rows_of(zz)

        @pl.when((zz >= z) & (z > 0))
        def _():
            z_copy(0, zz, p).wait_recv()
            acc[p, here, at, :] += z_in[0, zz, p]

        @pl.when((zz <= z) & (z < nz - 1))
        def _():
            z_copy(1, zz, p).wait_recv()
            acc[p, here, at, :] += z_in[1, zz, p]

        @pl.when(zz > z)
        def _():
            z_copy(0, zz, p).start()

        @pl.when(zz < z)
        def _():
            z_copy(1, zz, p).start()

    def settle(s, p):
        zz = place(s)

        def add_x():
            x_copy(s, p).wait_recv()
            acc[p, here, rows_of(zz), :] += x_in[s, p]

        if (s, p) in KEPT:
            pl.when(my_class == 0)(add_x)
        else:
            add_x()
        pass_on(zz, p)

    away_half(0)
    here_half(0)
    away_half(1)
    settle(0, 0)
    here_half(1)
    for s in range(nz):
        if s == nz - 1:
            @pl.when(my_class == 0)
            def _():
                for step in passed:
                    detour_copy(*step).wait_recv()
                    forward(*step).start()
                for step in KEPT:
                    detour_copy(*step).wait_recv()
                    acc[step[1], here, rows_of(place(s)), :] += detour_in[detour.index(step)]
        for p in range(2):
            if (s, p) != (0, 0):
                settle(s, p)
    for p in range(2):
        out_ref[:, p, :] = acc[p, here, rows_of(z), :] * norm_scale

    for s in range(nz):
        zz = place(s)
        for p in range(2):
            x_copy(s, p).wait_send()

            @pl.when(zz > z)
            def _():
                z_copy(0, zz, p).wait_send()

            @pl.when(zz < z)
            def _():
                z_copy(1, zz, p).wait_send()

    @pl.when(my_class == 0)
    def _():
        for step in passed:
            forward(*step).wait_send()

    for n in range(2):
        for k in range(2):
            core_copy(n, k).wait_send()
    for j in range(mine):
        left_copy(j).wait_send()
        others(lambda t: arrival(j, t).wait_send())


def by_kernel(left_local, right_local, norm_scale):
    idx, half = lax.axis_size("idx"), lax.axis_size("half")
    planes, per_idx, open_, inner = left_local.shape
    between = right_local.shape[3]
    mine = per_idx // half
    nx = 2
    nz = idx // nx
    group = idx * half
    block = open_ // group
    dma = pltpu.SemaphoreType.DMA
    sizes = (idx, half, mine, open_, inner, between, nx)
    complex_macs = mine * (inner * between * inner + open_ * inner * inner + open_ * inner * open_)
    out, _ = pl.pallas_call(
        functools.partial(kernel, sizes, norm_scale),
        out_shape=(
            jax.ShapeDtypeStruct((block, planes, open_), F32),
            jax.ShapeDtypeStruct((half, mine, planes, open_, inner), F32),
        ),
        in_specs=[pl.BlockSpec(memory_space=pl.ANY)] * 2,
        out_specs=(pl.BlockSpec(memory_space=pltpu.VMEM), pl.BlockSpec(memory_space=pl.ANY)),
        scratch_shapes=[
            pltpu.VMEM((mine, half, planes, inner, between), F32),
            pltpu.VMEM((half, planes, open_, inner), F32),
            pltpu.VMEM((3, 2, open_, inner), BF16),
            pltpu.VMEM((3, 2, open_, inner), BF16),
            pltpu.VMEM((3, inner, inner), F32),
            pltpu.VMEM((3, 2, inner, inner), BF16),
            pltpu.VMEM((planes, half * nx, nz * block, open_), F32),
            pltpu.VMEM((nx, planes, nz * block, open_), F32),
            pltpu.VMEM((nz, planes, block, open_), F32),
            pltpu.VMEM((2, nz, planes, block, open_), F32),
            pltpu.VMEM((len(DETOUR), block, open_), F32),
            dma((mine, group)), dma((mine, group)), dma((mine,)),
            dma((mine,)), dma((mine,)), dma((mine,)), dma((group + 1,)),
            dma((nx, 2)), dma((nx, 2)), dma((nz, planes)), dma((nz, planes)),
            dma((2, nz, planes)), dma((2, nz, planes)), dma((len(DETOUR),)), dma((len(DETOUR),)),
        ],
        compiler_params=pltpu.CompilerParams(
            collective_id=0, has_side_effects=True, vmem_limit_bytes=58 * 2**20
        ),
        cost_estimate=pl.CostEstimate(
            flops=18 * complex_macs, bytes_accessed=4 * (left_local.size + right_local.size), transcendentals=0
        ),
    )(left_local, right_local)
    return out


def swapped(x, axis, bit):
    return lax.ppermute(x, axis, [(i, i ^ 1 << bit) for i in range(lax.axis_size(axis))])


def complex_product(left_real, left_imag, right_real, right_imag, pattern):
    first_term = jnp.einsum(pattern, left_real, right_real, precision=HIGH)
    second_term = jnp.einsum(pattern, left_imag, right_imag, precision=HIGH)
    mixed_term = jnp.einsum(
        pattern, left_real + left_imag, right_real + right_imag, precision=HIGH
    )
    return (first_term - second_term, mixed_term - first_term - second_term)


def by_columns(left_local, right_local, norm_scale):
    columns = lax.all_to_all(right_local, "idx", split_axis=1, concat_axis=2, tiled=True)
    merged = jnp.stack(
        complex_product(left_local[0], left_local[1], columns[0], columns[1], "bmk,bkn->bmn")
    )
    half_cols = merged.shape[3] // 2
    half_index = lax.axis_index("half")
    outgoing = lax.dynamic_slice_in_dim(merged, (1 - half_index) * half_cols, half_cols, 3)
    own_slab = lax.dynamic_slice_in_dim(merged, half_index * half_cols, half_cols, 3)
    other_slab = swapped(outgoing, "half", 0)
    is_lower = half_index == 0
    first_pair = jnp.where(is_lower, own_slab, other_slab)
    second_pair = jnp.where(is_lower, other_slab, own_slab)
    real_part, imag_part = complex_product(
        first_pair[0], first_pair[1], second_pair[0], second_pair[1], "bmn,bon->mo"
    )
    return jnp.stack([real_part, imag_part], axis=1) * norm_scale


def on_device(left_factor, right_factor):
    left_local = left_factor[0]
    right_local = right_factor[0]
    batch, between = right_local.shape[1], right_local.shape[3]
    norm_scale = 1.0 / math.sqrt(2.0 * batch * between)
    idx, half = lax.axis_size("idx"), lax.axis_size("half")
    if half == 2 and idx == 2 * LINE and left_local.shape[1] % half == 0:
        return by_kernel(left_local, right_local, norm_scale)
    return lax.psum_scatter(
        by_columns(left_local, right_local, norm_scale),
        ("idx", "half"),
        scatter_dimension=0,
        tiled=True,
    )


def solution(mesh):
    return jax.shard_map(
        on_device,
        mesh=mesh,
        in_specs=(P("half", "cuts", "idx", None, None), P("half", "cuts", None, "idx", None)),
        out_specs=P(("idx", "half"), "cuts", None),
        check_vma=False,
    )
```
